32 devices in a mesh: harm: 8 (over z, x), slab: 4 (over y, core).
Axes of the slice: x: 2, y: 2, z: 4, core: 2. Of those that a mesh axis runs over, the one named last changes fastest.
Arguments:
- harmonics: float32 [8, 2, 5, 8, 2048], P('harm', None, None, 'slab'), may hold values from -4 to 4
- mean_flow: float32 [5, 8, 2048], P(None, 'slab'), may hold values from 0.5 to 13.5
- freq_index: int32 [8], P('harm'), may hold values from 1 to 8
- wall_mask: int32 [8, 2048], P('slab'), may hold values 0 or 1
- jacobian_x: float32 [5, 5], replicated, may hold values from -2.5 to 2.5
- jacobian_y: float32 [5, 5], replicated, may hold values from -2.5 to 2.5
Outputs:
- mean_next: float32 [5, 8, 2048], P(None, 'slab')
- harmonics_next: float32 [8, 2, 5, 8, 2048], P('harm', None, None, 'slab')
The draws below stay inside these ranges and needn't reach their ends.
All inputs are finite; a program needn't handle non-finite values. No bound on the sum of `wall_mask` on one device may be relied on, other than what follows from the above.
Results may differ from the reference program's by a relative error of at most 0.00018.
Values sent between devices are 32-bit elements; how exact they have to be, the bound alone decides.
A program may use at most 64 MiB of HBM per device.

```python
import jax
import jax.numpy as jnp
from jax import lax

NY = 32
NZ = 64
HARMONICS = 8
NX = 8


def draw_mean_flow(key, part):
    axial = jnp.arange(NX, dtype=jnp.float32) / (NX - 1)
    uniform_part = jax.random.uniform(key, (5, NX, NY * NZ), jnp.float32, 0.0, 1.0)
    profile = 1.0 + 2.0 * axial
    rough = 0.5 + uniform_part
    return profile[None, :, None] * rough


def touch_ends(drawn, own_key, low, largest):
    spot = [jax.random.randint(jax.random.fold_in(own_key, axis), (), 0, length) for axis, length in enumerate(drawn.shape)]
    widest = drawn.shape.index(max(drawn.shape))
    beside = spot[:widest] + [(spot[widest] + 1) % drawn.shape[widest]] + spot[widest + 1:]
    return drawn.at[tuple(spot)].set(low).at[tuple(beside)].set(largest)


def block_scale(own_key, extent, pieces, low, high):
    loudness, own = 1.0, jax.random.fold_in(own_key, 6)
    for axis_at, parts in pieces:
        draws = jnp.exp(jax.random.uniform(jax.random.fold_in(own, axis_at), (parts,), jnp.float32, low / len(pieces), high / len(pieces)))
        loudness = loudness * jnp.repeat(draws, extent[axis_at] // parts).reshape([-1 if axis == axis_at else 1 for axis in range(len(extent))])
    return loudness


def scatter_about(key, extent, scale, bound, cuts=(), kind=jnp.bfloat16):
    entries = scale * jax.random.normal(key, extent, jnp.float32)
    if cuts:
        entries = entries * block_scale(key, extent, cuts, -0.22, 0.18)
    return jnp.clip(entries, -bound, bound).astype(kind)


def setup_inputs(seed: int = 0) -> dict:
    splits = jax.random.split(jax.random.key(seed), 7)
    return {
        "harmonics": scatter_about(splits[0], (HARMONICS, 2, 5, NX, NY * NZ), 0.3, 4.0, ((0, 8), (3, 4)), jnp.float32),
        "mean_flow": draw_mean_flow(jax.random.fold_in(splits[6], 71), 0),
        "freq_index": touch_ends(jax.random.randint(splits[2], (HARMONICS,), 1, 9), jax.random.fold_in(splits[2], 1), 1, 8).astype(jnp.int32),
        "wall_mask": touch_ends((jax.random.randint(splits[3], (NX, NY * NZ), 0, 8) < 1).astype(jnp.int32), jax.random.fold_in(splits[3], 1), 0, 1),
        "jacobian_x": scatter_about(splits[4], (5, 5), 5 ** -0.5, 2.5, (), jnp.float32),
        "jacobian_y": scatter_about(splits[5], (5, 5), 5 ** -0.5, 2.5, (), jnp.float32),
    }


EPS_FOURTH = 0.05
COURANT = 0.9
OMEGA_BASE = 0.25
WALL_RATE = 2.0
HUB_RADIUS = 0.5
SECTION_RATES = (0.25, 1.0 / 3.0, 0.5, 1.0)
STRESS_PAIRS = ((1, 1), (1, 2), (1, 3), (2, 2), (2, 3), (3, 3), (4, 1), (4, 2), (4, 3))

def apply_matrix(matrix, values):
    return jnp.einsum('ab,...bxp->...axp', matrix, values, precision=lax.Precision.HIGHEST)

def diff_across(values):
    return (jnp.roll(values, -NZ, axis=-1) - jnp.roll(values, NZ, axis=-1)) * 0.5

def fourth_across(values):
    return jnp.roll(values, -2 * NZ, axis=-1) - 4.0 * jnp.roll(values, -NZ, axis=-1) + 6.0 * values - 4.0 * jnp.roll(values, NZ, axis=-1) + jnp.roll(values, 2 * NZ, axis=-1)

def diff_along(padded):
    return (padded[..., 3:-1, :] - padded[..., 1:-3, :]) * 0.5

def fourth_along(padded):
    return padded[..., 4:, :] - 4.0 * padded[..., 3:-1, :] + 6.0 * padded[..., 2:-2, :] - 4.0 * padded[..., 1:-3, :] + padded[..., :-4, :]

def harmonic_residual(harm_pad, momentum_pad, omega, wall_cells, jac_x, jac_y):
    center = harm_pad[..., 2:-2, :]
    flux_x = apply_matrix(jac_x, harm_pad * momentum_pad)
    flux_y = apply_matrix(jac_y, center)
    rotation = jnp.stack([center[..., 1, :, :, :], -center[..., 0, :, :, :]], axis=-4) * omega
    return rotation - diff_along(flux_x) - diff_across(flux_y) - EPS_FOURTH * (fourth_along(harm_pad) + fourth_across(center)) - WALL_RATE * wall_cells * center

def stresses(values):
    fields = []
    for first, second in STRESS_PAIRS:
        product = values[..., first, :, :] * values[..., second, :, :]
        fields.append(0.5 * lax.optimization_barrier(jnp.sum(product, axis=tuple(range(product.ndim - 2)))))
    return jnp.stack(fields, axis=0)

def forcing(stress_pad, radius):
    center = stress_pad[:, 1:-1, :]
    grad_x = (stress_pad[:, 2:, :] - stress_pad[:, :-2, :]) * 0.5
    grad_y = diff_across(center)
    first = -grad_x[0] - grad_y[1]
    second = -grad_x[1] - grad_y[3] - 2.0 * center[4] / radius
    third = -grad_x[2] - grad_y[4] + (center[3] - center[5]) / radius
    fourth = -grad_x[6] - grad_y[7] - center[8] / radius
    return jnp.stack([first, second, third, fourth], axis=0)

def mean_residual(mean_pad, forcing_terms, jac_x, jac_y):
    center = mean_pad[:, 2:-2, :]
    residual = -diff_along(apply_matrix(jac_x, mean_pad)) - diff_across(apply_matrix(jac_y, center)) - EPS_FOURTH * (fourth_along(mean_pad) + fourth_across(center))
    zeros_row = jnp.zeros_like(forcing_terms[:1])
    return residual + jnp.concatenate([zeros_row, forcing_terms], axis=0)

def reference(harmonics, mean_flow, freq_index, wall_mask, jacobian_x, jacobian_y):
    plane_count = mean_flow.shape[2]
    radius = HUB_RADIUS + ((jnp.arange(plane_count) % NZ).astype(jnp.float32) + 0.5) / NZ
    wall_cells = wall_mask.astype(jnp.float32)
    omegas = OMEGA_BASE * freq_index.astype(jnp.float32)
    speed_total = jnp.sum(mean_flow[1] * mean_flow[1])
    time_step = COURANT / (1.0 + jnp.sqrt(speed_total / (NX * NY * NZ)))
    harm_now, mean_now = (harmonics, mean_flow)
    for section_rate in SECTION_RATES:
        mean_pad = jnp.pad(mean_now, ((0, 0), (2, 2), (0, 0)))

        def single_residual(member):
            single, omega_one = member
            padded = jnp.pad(single, ((0, 0), (0, 0), (2, 2), (0, 0)))
            return harmonic_residual(padded, mean_pad[1], omega_one, wall_cells, jacobian_x, jacobian_y)
        harm_res = lax.map(single_residual, (harm_now, omegas))
        stress_pad = jnp.pad(stresses(harm_now), ((0, 0), (1, 1), (0, 0)))
        mean_res = mean_residual(mean_pad, forcing(stress_pad, radius), jacobian_x, jacobian_y)
        harm_now = harmonics + section_rate * time_step * harm_res
        mean_now = mean_flow + section_rate * time_step * mean_res
    return (mean_now, harm_now)
```

```python
import functools

import jax
import jax.numpy as jnp
from jax import lax
from jax.experimental import pallas as pl
from jax.experimental.pallas import tpu as pltpu
from jax.sharding import PartitionSpec as P

NZ = 64


EPS_FOURTH = 0.05
COURANT = 0.9
OMEGA_BASE = 0.25
WALL_RATE = 2.0
HUB_RADIUS = 0.5
SECTION_RATES = (0.25, 1.0 / 3.0, 0.5, 1.0)
STRESS_PAIRS = ((1, 1), (1, 2), (1, 3), (2, 2), (2, 3), (3, 3), (4, 1), (4, 2), (4, 3))


def with_halo(cells, sides, width):
    for axis, dim in sides:
        count = lax.axis_size(axis)
        ends = count - 1
        head = lax.slice_in_dim(cells, 0, width, axis=dim)
        tail = lax.slice_in_dim(cells, cells.shape[dim] - width, cells.shape[dim], axis=dim)
        cells = jnp.concatenate(
            [
                lax.ppermute(tail, axis, [(i, (i + 1) % count) for i in range(ends)]),
                cells,
                lax.ppermute(head, axis, [((i + 1) % count, i) for i in range(ends)]),
            ],
            axis=dim,
        )
    return cells


def apply_matrix(matrix, values):
    return jnp.einsum("ab,...bxp->...axp", matrix, values, precision=lax.Precision.HIGHEST)


def diff_across(values):
    return (jnp.roll(values, -NZ, axis=-1) - jnp.roll(values, NZ, axis=-1)) * 0.5


def fourth_across(values):
    return (
        jnp.roll(values, -2 * NZ, axis=-1)
        - 4.0 * jnp.roll(values, -NZ, axis=-1)
        + 6.0 * values
        - 4.0 * jnp.roll(values, NZ, axis=-1)
        + jnp.roll(values, 2 * NZ, axis=-1)
    )


def diff_along(padded):
    return (padded[..., 3:-1, :] - padded[..., 1:-3, :]) * 0.5


def fourth_along(padded):
    return (
        padded[..., 4:, :]
        - 4.0 * padded[..., 3:-1, :]
        + 6.0 * padded[..., 2:-2, :]
        - 4.0 * padded[..., 1:-3, :]
        + padded[..., :-4, :]
    )


def harmonic_residual(harm_pad, momentum_pad, omegas, wall_cells, jac_x, jac_y):
    center = harm_pad[..., 2:-2, :]
    flux_x = apply_matrix(jac_x, harm_pad * momentum_pad)
    flux_y = apply_matrix(jac_y, center)
    rotation = jnp.stack([center[..., 1, :, :, :], -center[..., 0, :, :, :]], axis=-4) * omegas
    return (
        rotation
        - diff_along(flux_x)
        - diff_across(flux_y)
        - EPS_FOURTH * (fourth_along(harm_pad) + fourth_across(center))
        - WALL_RATE * wall_cells * center
    )


def stresses(values):
    fields = []
    for first, second in STRESS_PAIRS:
        product = values[..., first, :, :] * values[..., second, :, :]
        fields.append(0.5 * jnp.sum(product, axis=tuple(range(product.ndim - 2))))
    return jnp.stack(fields, axis=0)


def forcing(stress_pad, radius):
    center = stress_pad[:, 1:-1, :]
    grad_x = (stress_pad[:, 2:, :] - stress_pad[:, :-2, :]) * 0.5
    grad_y = diff_across(center)
    first = -grad_x[0] - grad_y[1]
    second = -grad_x[1] - grad_y[3] - 2.0 * center[4] / radius
    third = -grad_x[2] - grad_y[4] + (center[3] - center[5]) / radius
    fourth = -grad_x[6] - grad_y[7] - center[8] / radius
    return jnp.stack([first, second, third, fourth], axis=0)


def mean_residual(mean_pad, forcing_terms, jac_x, jac_y):
    center = mean_pad[:, 2:-2, :]
    residual = (
        -diff_along(apply_matrix(jac_x, mean_pad))
        - diff_across(apply_matrix(jac_y, center))
        - EPS_FOURTH * (fourth_along(mean_pad) + fourth_across(center))
    )
    zeros_row = jnp.zeros_like(forcing_terms[:1])
    return residual + jnp.concatenate([zeros_row, forcing_terms], axis=0)


def shards(harmonics, mean_flow, freq_index, wall_mask, jacobian_x, jacobian_y):
    owned = harmonics.shape[0]
    slab_cells = mean_flow.shape[1]
    plane_count = mean_flow.shape[2]
    radius = HUB_RADIUS + ((jnp.arange(plane_count) % NZ).astype(jnp.float32) + 0.5) / NZ
    wall_cells = wall_mask.astype(jnp.float32)
    omegas = (OMEGA_BASE * freq_index.astype(jnp.float32)).reshape(owned, 1, 1, 1, 1)
    speed_total = lax.psum(jnp.sum(mean_flow[1] * mean_flow[1]), "slab")
    cell_count = slab_cells * lax.axis_size("slab") * plane_count
    time_step = COURANT / (1.0 + jnp.sqrt(speed_total / cell_count))
    harm_now, mean_now = (harmonics, mean_flow)
    for section_rate in SECTION_RATES:
        stacked = jnp.concatenate(
            [harm_now.reshape(owned * 2, 5, slab_cells, plane_count), mean_now[None]], axis=0
        )
        padded = with_halo(stacked, (("slab", 2),), 2)
        harm_pad = padded[: 2 * owned].reshape(owned, 2, 5, slab_cells + 4, plane_count)
        mean_pad = padded[2 * owned]
        harm_res = harmonic_residual(
            harm_pad, mean_pad[1], omegas, wall_cells, jacobian_x, jacobian_y
        )
        partial_terms = forcing(stresses(harm_pad[..., 1:-1, :]), radius)
        forcing_terms = lax.psum(partial_terms, "harm")
        mean_res = mean_residual(mean_pad, forcing_terms, jacobian_x, jacobian_y)
        harm_now = harmonics + section_rate * time_step * harm_res
        mean_now = mean_flow + section_rate * time_step * mean_res
    return (mean_now, harm_now)


MESH_ID = pl.DeviceIdType.MESH
LANES = 128
ROWS = 8
F32 = jnp.float32


def swap_bit(pair, stride, bit):
    low, high = pair
    return (
        jnp.where(bit == 0, low, pltpu.roll(high, stride, 1)),
        jnp.where(bit == 0, pltpu.roll(low, LANES - stride, 1), high),
    )


def radial_kernel(
    dims, h_ref, m_ref, f_ref, w_ref, jx_ref, jy_ref, mo_ref, ho_ref,
    rows, send, recv, mrecv, state, first, omega, mean, mean0, back, home,
    hs_sem, hr_sem, ms_sem, mr_sem, bs_sem, br_sem,
):
    nh, ns, nvar, cells, tiles = dims
    nd = nh * ns
    mh, ms = lax.axis_index("harm"), lax.axis_index("slab")
    me = mh * ns + ms
    nx = ns * cells

    barrier = pltpu.get_barrier_semaphore()

    def greet(o, _):
        d = lax.rem(me + o, nd)
        pl.semaphore_signal(
            barrier, inc=1, device_id=(d // ns, lax.rem(d, ns)), device_id_type=MESH_ID
        )
        return 0

    lax.fori_loop(1, nd, greet, 0)

    lane_all = lax.broadcasted_iota(jnp.int32, (nd, LANES), 1)
    low_bit = lane_all & 1
    high_bit = (lane_all >> 2) & 1

    def place(at, value):
        rows[pl.ds(cells * at, cells), :] = value

    for a in range(nvar):
        for c in range(2):
            place(2 * a + c, h_ref[0, c, a])
    place(2 * nvar, m_ref[nvar - 1])
    place(2 * nvar + 1, w_ref[...].astype(F32))
    for a in range(nvar - 1):
        place(2 * nvar + 2 + a, m_ref[a])

    def block_of(g):
        return g if g < nvar else g + 1

    for grp in range(4):
        mat = jnp.concatenate(
            [rows[ROWS * grp : ROWS * grp + ROWS, LANES * t : LANES * t + LANES] for t in range(tiles)],
            axis=0,
        )
        turned = mat.T
        part = [[turned[nd * (2 * i + j) : nd * (2 * i + j) + nd] for j in range(2)] for i in range(2)]
        cols = [swap_bit((part[0][j], part[1][j]), 4, high_bit) for j in range(2)]
        for g1 in range(2):
            outs = swap_bit((cols[0][g1], cols[1][g1]), 1, low_bit)
            for g0 in range(2):
                send[:, block_of(2 * grp + g1), g0, :] = outs[g0]
    speed = m_ref[1]
    partial_sum = jnp.sum(jnp.sum(speed * speed, axis=1, keepdims=True), axis=0, keepdims=True)
    rate_own = jnp.full((1, 1), 0.25 * f_ref[0].astype(F32), F32)
    send[:, nvar, 0, :] = jnp.broadcast_to(rate_own, (nd, LANES))
    send[:, nvar, 1, :] = jnp.broadcast_to(partial_sum, (nd, LANES))

    recv[mh, ms] = send[me, 0 : nvar + 1]
    mrecv[ms] = send[me, nvar + 1 : nvar + 4]

    pl.semaphore_wait(barrier, nd - 1)

    def out_copy(d):
        return pltpu.make_async_remote_copy(
            src_ref=send.at[d, pl.ds(0, nvar + 1)],
            dst_ref=recv.at[mh, ms],
            send_sem=hs_sem.at[d],
            recv_sem=hr_sem.at[me],
            device_id=(d // ns, lax.rem(d, ns)),
            device_id_type=MESH_ID,
        )

    def in_copy(d):
        return pltpu.make_async_remote_copy(
            src_ref=send.at[d, pl.ds(0, nvar + 1)],
            dst_ref=recv.at[d // ns, lax.rem(d, ns)],
            send_sem=hs_sem.at[d],
            recv_sem=hr_sem.at[d],
            device_id=(d // ns, lax.rem(d, ns)),
            device_id_type=MESH_ID,
        )

    def mean_out(s):
        return pltpu.make_async_remote_copy(
            src_ref=send.at[mh * ns + s, pl.ds(nvar + 1, 3)],
            dst_ref=mrecv.at[ms],
            send_sem=ms_sem.at[s],
            recv_sem=mr_sem.at[ms],
            device_id=(mh, s),
            device_id_type=MESH_ID,
        )

    def mean_in(s):
        return pltpu.make_async_remote_copy(
            src_ref=send.at[mh * ns + s, pl.ds(nvar + 1, 3)],
            dst_ref=mrecv.at[s],
            send_sem=ms_sem.at[s],
            recv_sem=mr_sem.at[s],
            device_id=(mh, s),
            device_id_type=MESH_ID,
        )

    def go(o, _):
        out_copy(lax.rem(me + o, nd)).start()
        return 0

    def go_mean(o, _):
        mean_out(lax.rem(ms + o, ns)).start()
        return 0

    def land(o, _):
        in_copy(lax.rem(me + o, nd)).wait_recv()
        return 0

    def land_mean(o, _):
        mean_in(lax.rem(ms + o, ns)).wait_recv()
        return 0

    lax.fori_loop(1, nd, go, 0)
    lax.fori_loop(1, ns, go_mean, 0)
    lax.fori_loop(1, nd, land, 0)
    lax.fori_loop(1, ns, land_mean, 0)

    lane = lax.broadcasted_iota(jnp.int32, (nx, LANES), 1)
    cell = lax.broadcasted_iota(jnp.int32, (nx, LANES), 0)
    second = (lane >> 1) & 1
    is_real = second == 0

    def other(value):
        return jnp.where(is_real, pltpu.roll(value, LANES - 2, 1), pltpu.roll(value, 2, 1))

    def spread(value):
        turned = other(value)
        return jnp.where(is_real, value, turned), jnp.where(is_real, turned, value)

    def assemble(k, _):
        for s in range(ns):
            for a in range(nvar):
                got = recv[k, s, a]
                state[k, a, cells * s : cells * s + cells, :] = got
                first[k, a, cells * s : cells * s + cells, :] = got
        omega[k] = jnp.broadcast_to(recv[k, 0, nvar, 0:1, :], (nx, LANES))
        return 0

    lax.fori_loop(0, nh, assemble, 0)
    packed = []
    for b in range(3):
        for s in range(ns):
            mean[b, cells * s : cells * s + cells, :] = mrecv[s, b]
        packed.append(mean[b])
    m4, wall = spread(packed[0])
    m0, m1 = spread(packed[1])
    m2, m3 = spread(packed[2])
    for a, value in enumerate((m0, m1, m2, m3, m4)):
        mean[a] = value
        mean0[a] = value
    total = recv[0, 0, nvar, 1:2, :]
    for s in range(1, ns):
        total = total + recv[0, s, nvar, 1:2, :]
    count = nx * tiles * LANES
    time_step = jnp.broadcast_to(0.9 / (1.0 + jnp.sqrt(total / count)), (nx, LANES))
    wall2 = 2.0 * wall
    z = (lane & 1) * nd + me
    radius = 0.5 + (z.astype(F32) + 0.5) / (2 * nd)
    inv_r = 1.0 / radius

    mp1 = jnp.where(cell < nx - 1, 1.0, 0.0).astype(F32)
    mm1 = jnp.where(cell > 0, 1.0, 0.0).astype(F32)
    mp2 = jnp.where(cell < nx - 2, 1.0, 0.0).astype(F32)
    mm2 = jnp.where(cell > 1, 1.0, 0.0).astype(F32)

    def xp(v, n):
        return pltpu.roll(v, nx - n, 0)

    def xm(v, n):
        return pltpu.roll(v, n, 0)

    def yp(v, n):
        return pltpu.roll(v, LANES - 4 * n, 1)

    def ym(v, n):
        return pltpu.roll(v, 4 * n, 1)

    def pieces(v, fwd, bwd):
        xp1, xm1 = xp(v, 1), xm(v, 1)
        yp1, ym1 = yp(v, 1), ym(v, 1)
        fourth = (
            mp2 * xp(v, 2) + mm2 * xm(v, 2) + 12.0 * v + yp(v, 2) + ym(v, 2)
            - 4.0 * (mp1 * xp1 + mm1 * xm1 + yp1 + ym1)
        )
        return fwd * xp1 - bwd * xm1, yp1 - ym1, fourth

    def mix(us, vs, a):
        flux = jx_ref[a, 0] * us[0]
        for b in range(1, nvar):
            flux = flux + jx_ref[a, b] * us[b]
        for b in range(nvar):
            flux = flux + jy_ref[a, b] * vs[b]
        return 0.5 * flux

    pairs = ((1, 1), (1, 2), (1, 3), (2, 2), (2, 3), (3, 3), (4, 1), (4, 2), (4, 3))

    def section(i, _):
        rate = jnp.where(i == 0, 0.25, jnp.where(i == 1, 1.0 / 3.0, jnp.where(i == 2, 0.5, 1.0))).astype(F32)
        step = rate * time_step
        mc = mean[1]
        fwd = mp1 * xp(mc, 1)
        bwd = mm1 * xm(mc, 1)

        def one(k, acc):
            hs = [state[k, a] for a in range(nvar)]
            acc = tuple(s + hs[p] * hs[q] for s, (p, q) in zip(acc, pairs))
            om = jnp.where(is_real, omega[k], -omega[k])
            got = [pieces(h, fwd, bwd) for h in hs]
            us, vs = [g[0] for g in got], [g[1] for g in got]
            for a in range(nvar):
                res = om * other(hs[a]) - mix(us, vs, a) - 0.05 * got[a][2] - wall2 * hs[a]
                state[k, a] = first[k, a] + step * res
            return acc

        zero = jnp.zeros((nx, LANES), F32)
        acc = lax.fori_loop(0, nh, one, (zero,) * len(pairs))
        s = [0.5 * (v + other(v)) for v in acc]

        def gx(v):
            return 0.5 * (mp1 * xp(v, 1) - mm1 * xm(v, 1))

        def gy(v):
            return 0.5 * (yp(v, 1) - ym(v, 1))

        force = (
            zero,
            -gx(s[0]) - gy(s[1]),
            -gx(s[1]) - gy(s[3]) - 2.0 * s[4] * inv_r,
            -gx(s[2]) - gy(s[4]) + (s[3] - s[5]) * inv_r,
            -gx(s[6]) - gy(s[7]) - s[8] * inv_r,
        )
        means = [mean[a] for a in range(nvar)]
        got = [pieces(m, mp1, mm1) for m in means]
        us, vs = [g[0] for g in got], [g[1] for g in got]
        for a in range(nvar):
            res = force[a] - mix(us, vs, a) - 0.05 * got[a][2]
            mean[a] = mean0[a] + step * res
        return 0

    lax.fori_loop(0, 4, section, 0)

    def join(even, odd):
        return jnp.where(is_real, even, odd)

    packs = (mean[4], join(mean[0], mean[1]), join(mean[2], mean[3]))

    def leave(k, _):
        for s in range(ns):
            for a in range(nvar):
                back[k, s, a] = state[k, a, cells * s : cells * s + cells, :]
            for b in range(3):
                back[k, s, nvar + b] = packs[b][cells * s : cells * s + cells, :]
        return 0

    lax.fori_loop(0, nh, leave, 0)
    home[me] = back[mh, ms]

    def back_copy(d, slot):
        return pltpu.make_async_remote_copy(
            src_ref=back.at[d // ns, lax.rem(d, ns)],
            dst_ref=home.at[slot],
            send_sem=bs_sem.at[d],
            recv_sem=br_sem.at[slot],
            device_id=(d // ns, lax.rem(d, ns)),
            device_id_type=MESH_ID,
        )

    def go_back(o, _):
        d = lax.rem(me + o, nd)
        back_copy(d, me).start()
        return 0

    def land_back(o, _):
        d = lax.rem(me + o, nd)
        back_copy(d, d).wait_recv()
        return 0

    lax.fori_loop(1, nd, go_back, 0)
    lax.fori_loop(1, nd, land_back, 0)

    for grp in range(4):
        cols = []
        for g1 in range(2):
            cols.append(swap_bit([home[:, 2 * grp + g1, g0, :] for g0 in range(2)], 1, low_bit))
        part = [swap_bit((cols[0][j], cols[1][j]), 4, high_bit) for j in range(2)]
        mat = jnp.concatenate([part[j][i] for i in range(2) for j in range(2)], axis=0)
        turned = mat.T
        for t in range(tiles):
            rows[ROWS * grp : ROWS * grp + ROWS, LANES * t : LANES * t + LANES] = turned[
                ROWS * t : ROWS * t + ROWS
            ]

    def take(at):
        return rows[pl.ds(cells * at, cells), :]

    for a in range(nvar):
        for c in range(2):
            ho_ref[0, c, a] = take(2 * a + c)
    mo_ref[nvar - 1] = take(2 * nvar)
    for a in range(nvar - 1):
        mo_ref[a] = take(2 * nvar + 2 + a)

    def sent(o, _):
        d = lax.rem(me + o, nd)
        out_copy(d).wait_send()
        back_copy(d, me).wait_send()
        return 0

    def sent_mean(o, _):
        mean_out(lax.rem(ms + o, ns)).wait_send()
        return 0

    lax.fori_loop(1, nd, sent, 0)
    lax.fori_loop(1, ns, sent_mean, 0)


def radial_shards(nh, ns, harmonics, mean_flow, freq_index, wall_mask, jacobian_x, jacobian_y):
    nvar, cells, planes = mean_flow.shape
    nd, nx = nh * ns, ns * cells
    vmem = pl.BlockSpec(memory_space=pltpu.VMEM)
    smem = pl.BlockSpec(memory_space=pltpu.SMEM)
    dims = (nh, ns, nvar, cells, planes // LANES)
    field = (nx, LANES)
    piece = (cells, LANES)
    return pl.pallas_call(
        functools.partial(radial_kernel, dims),
        out_shape=(
            jax.ShapeDtypeStruct(mean_flow.shape, F32),
            jax.ShapeDtypeStruct(harmonics.shape, F32),
        ),
        in_specs=[vmem, vmem, smem, vmem, smem, smem],
        out_specs=(vmem, vmem),
        scratch_shapes=[
            pltpu.VMEM((4 * ROWS, planes), F32),
            pltpu.VMEM((nd, nvar + 4, *piece), F32),
            pltpu.VMEM((nh, ns, nvar + 1, *piece), F32),
            pltpu.VMEM((ns, 3, *piece), F32),
            pltpu.VMEM((nh, nvar, *field), F32),
            pltpu.VMEM((nh, nvar, *field), F32),
            pltpu.VMEM((nh, *field), F32),
            pltpu.VMEM((nvar, *field), F32),
            pltpu.VMEM((nvar, *field), F32),
            pltpu.VMEM((nh, ns, nvar + 3, *piece), F32),
            pltpu.VMEM((nd, nvar + 3, *piece), F32),
            pltpu.SemaphoreType.DMA((nd,)),
            pltpu.SemaphoreType.DMA((nd,)),
            pltpu.SemaphoreType.DMA((ns,)),
            pltpu.SemaphoreType.DMA((ns,)),
            pltpu.SemaphoreType.DMA((nd,)),
            pltpu.SemaphoreType.DMA((nd,)),
        ],
        compiler_params=pltpu.CompilerParams(collective_id=0, has_side_effects=True),
    )(harmonics, mean_flow, freq_index, wall_mask, jacobian_x, jacobian_y)


def fits_radial(nh, ns, harmonics, mean_flow):
    owned, parts, nvar, cells, planes = harmonics.shape
    return (
        NZ == 2 * nh * ns
        and LANES == 2 * NZ
        and (owned, parts, nvar, cells) == (1, 2, 5, 2)
        and ns * cells == ROWS
        and planes == 16 * LANES
    )


def either(nh, ns, harmonics, mean_flow, *rest):
    if fits_radial(nh, ns, harmonics, mean_flow):
        return radial_shards(nh, ns, harmonics, mean_flow, *rest)
    return shards(harmonics, mean_flow, *rest)


def solution(mesh):
    placed = (
        P("harm", None, None, "slab", None),
        P(None, "slab", None),
        P("harm"),
        P("slab", None),
        P(),
        P(),
    )
    return jax.shard_map(
        functools.partial(either, mesh.shape["harm"], mesh.shape["slab"]),
        mesh=mesh,
        in_specs=placed,
        out_specs=(P(None, "slab", None), P("harm", None, None, "slab", None)),
        check_vma=False,
    )
```

```python
import functools

import jax
import jax.numpy as jnp
from jax import lax
from jax.experimental import pallas as pl
from jax.experimental.pallas import tpu as pltpu
from jax.sharding import PartitionSpec as P

NZ = 64


EPS_FOURTH = 0.05
COURANT = 0.9
OMEGA_BASE = 0.25
WALL_RATE = 2.0
HUB_RADIUS = 0.5
SECTION_RATES = (0.25, 1.0 / 3.0, 0.5, 1.0)
STRESS_PAIRS = ((1, 1), (1, 2), (1, 3), (2, 2), (2, 3), (3, 3), (4, 1), (4, 2), (4, 3))


def with_halo(cells, sides, width):
    for axis, dim in sides:
        count = lax.axis_size(axis)
        ends = count - 1
        head = lax.slice_in_dim(cells, 0, width, axis=dim)
        tail = lax.slice_in_dim(cells, cells.shape[dim] - width, cells.shape[dim], axis=dim)
        cells = jnp.concatenate(
            [
                lax.ppermute(tail, axis, [(i, (i + 1) % count) for i in range(ends)]),
                cells,
                lax.ppermute(head, axis, [((i + 1) % count, i) for i in range(ends)]),
            ],
            axis=dim,
        )
    return cells


def apply_matrix(matrix, values):
    return jnp.einsum("ab,...bxp->...axp", matrix, values, precision=lax.Precision.HIGHEST)


def diff_across(values):
    return (jnp.roll(values, -NZ, axis=-1) - jnp.roll(values, NZ, axis=-1)) * 0.5


def fourth_across(values):
    return (
        jnp.roll(values, -2 * NZ, axis=-1)
        - 4.0 * jnp.roll(values, -NZ, axis=-1)
        + 6.0 * values
        - 4.0 * jnp.roll(values, NZ, axis=-1)
        + jnp.roll(values, 2 * NZ, axis=-1)
    )


def diff_along(padded):
    return (padded[..., 3:-1, :] - padded[..., 1:-3, :]) * 0.5


def fourth_along(padded):
    return (
        padded[..., 4:, :]
        - 4.0 * padded[..., 3:-1, :]
        + 6.0 * padded[..., 2:-2, :]
        - 4.0 * padded[..., 1:-3, :]
        + padded[..., :-4, :]
    )


def harmonic_residual(harm_pad, momentum_pad, omegas, wall_cells, jac_x, jac_y):
    center = harm_pad[..., 2:-2, :]
    flux_x = apply_matrix(jac_x, harm_pad * momentum_pad)
    flux_y = apply_matrix(jac_y, center)
    rotation = jnp.stack([center[..., 1, :, :, :], -center[..., 0, :, :, :]], axis=-4) * omegas
    return (
        rotation
        - diff_along(flux_x)
        - diff_across(flux_y)
        - EPS_FOURTH * (fourth_along(harm_pad) + fourth_across(center))
        - WALL_RATE * wall_cells * center
    )


def stresses(values):
    fields = []
    for first, second in STRESS_PAIRS:
        product = values[..., first, :, :] * values[..., second, :, :]
        fields.append(0.5 * jnp.sum(product, axis=tuple(range(product.ndim - 2))))
    return jnp.stack(fields, axis=0)


def forcing(stress_pad, radius):
    center = stress_pad[:, 1:-1, :]
    grad_x = (stress_pad[:, 2:, :] - stress_pad[:, :-2, :]) * 0.5
    grad_y = diff_across(center)
    first = -grad_x[0] - grad_y[1]
    second = -grad_x[1] - grad_y[3] - 2.0 * center[4] / radius
    third = -grad_x[2] - grad_y[4] + (center[3] - center[5]) / radius
    fourth = -grad_x[6] - grad_y[7] - center[8] / radius
    return jnp.stack([first, second, third, fourth], axis=0)


def mean_residual(mean_pad, forcing_terms, jac_x, jac_y):
    center = mean_pad[:, 2:-2, :]
    residual = (
        -diff_along(apply_matrix(jac_x, mean_pad))
        - diff_across(apply_matrix(jac_y, center))
        - EPS_FOURTH * (fourth_along(mean_pad) + fourth_across(center))
    )
    zeros_row = jnp.zeros_like(forcing_terms[:1])
    return residual + jnp.concatenate([zeros_row, forcing_terms], axis=0)


def shards(harmonics, mean_flow, freq_index, wall_mask, jacobian_x, jacobian_y):
    owned = harmonics.shape[0]
    slab_cells = mean_flow.shape[1]
    plane_count = mean_flow.shape[2]
    radius = HUB_RADIUS + ((jnp.arange(plane_count) % NZ).astype(jnp.float32) + 0.5) / NZ
    wall_cells = wall_mask.astype(jnp.float32)
    omegas = (OMEGA_BASE * freq_index.astype(jnp.float32)).reshape(owned, 1, 1, 1, 1)
    speed_total = lax.psum(jnp.sum(mean_flow[1] * mean_flow[1]), "slab")
    cell_count = slab_cells * lax.axis_size("slab") * plane_count
    time_step = COURANT / (1.0 + jnp.sqrt(speed_total / cell_count))
    harm_now, mean_now = (harmonics, mean_flow)
    for section_rate in SECTION_RATES:
        stacked = jnp.concatenate(
            [harm_now.reshape(owned * 2, 5, slab_cells, plane_count), mean_now[None]], axis=0
        )
        padded = with_halo(stacked, (("slab", 2),), 2)
        harm_pad = padded[: 2 * owned].reshape(owned, 2, 5, slab_cells + 4, plane_count)
        mean_pad = padded[2 * owned]
        harm_res = harmonic_residual(
            harm_pad, mean_pad[1], omegas, wall_cells, jacobian_x, jacobian_y
        )
        partial_terms = forcing(stresses(harm_pad[..., 1:-1, :]), radius)
        forcing_terms = lax.psum(partial_terms, "harm")
        mean_res = mean_residual(mean_pad, forcing_terms, jacobian_x, jacobian_y)
        harm_now = harmonics + section_rate * time_step * harm_res
        mean_now = mean_flow + section_rate * time_step * mean_res
    return (mean_now, harm_now)


MESH_ID = pl.DeviceIdType.MESH
LANES = 128
ROWS = 8
F32 = jnp.float32


def swap_bit(pair, stride, bit):
    low, high = pair
    return (
        jnp.where(bit == 0, low, pltpu.roll(high, stride, 1)),
        jnp.where(bit == 0, pltpu.roll(low, LANES - stride, 1), high),
    )


def radial_kernel(
    dims, h_any, m_any, f_ref, w_any, jx_ref, jy_ref, mo_ref, ho_ref,
    h_ref, m_ref, w_ref, in_sem, rows, send, recv, mrecv, state, first, omega, mean, mean0, back, home,
    hs_sem, hr_sem, ms_sem, mr_sem, bs_sem, br_sem,
):
    nh, ns, nvar, cells, tiles = dims
    nd = nh * ns
    mh, ms = lax.axis_index("harm"), lax.axis_index("slab")
    me = mh * ns + ms
    nx = ns * cells

    barrier = pltpu.get_barrier_semaphore()

    def flip(index, bits):
        out = index
        weight = 1
        while weight <= bits:
            if bits & weight:
                out = out + weight * (1 - 2 * lax.rem(index // weight, 2))
            weight *= 2
        return out

    def flip_by(index, bits):
        out = index
        weight = 1
        while weight < nh:
            out = out + lax.rem(bits // weight, 2) * weight * (1 - 2 * lax.rem(index // weight, 2))
            weight *= 2
        return out

    def reach(offset):
        oh, os = offset
        return min(oh >> 1, 2) + (oh & 1) + (os >> 1) + 0.3 * (os & 1)

    far_first = sorted(
        [(oh, os) for oh in range(nh) for os in range(ns) if oh or os], key=reach, reverse=True
    )
    for oh, os in far_first:
        pl.semaphore_signal(
            barrier, inc=1, device_id=(flip(mh, oh), flip(ms, os)), device_id_type=MESH_ID
        )
    loads = [
        pltpu.make_async_copy(src, dst, in_sem.at[i])
        for i, (src, dst) in enumerate(((h_any, h_ref), (m_any, m_ref), (w_any, w_ref)))
    ]
    for load in loads:
        load.start()
    for load in loads:
        load.wait()

    lane_all = lax.broadcasted_iota(jnp.int32, (nd, LANES), 1)
    low_bit = lane_all & 1
    high_bit = (lane_all >> 2) & 1

    def place(at, value):
        rows[pl.ds(cells * at, cells), :] = value

    for a in range(nvar):
        for c in range(2):
            place(2 * a + c, h_ref[0, c, a])
    place(2 * nvar, m_ref[nvar - 1])
    place(2 * nvar + 1, w_ref[...].astype(F32))
    for a in range(nvar - 1):
        place(2 * nvar + 2 + a, m_ref[a])

    def block_of(g):
        return g if g < nvar else g + 1

    for grp in range(4):
        mat = jnp.concatenate(
            [rows[ROWS * grp : ROWS * grp + ROWS, LANES * t : LANES * t + LANES] for t in range(tiles)],
            axis=0,
        )
        turned = mat.T
        part = [[turned[nd * (2 * i + j) : nd * (2 * i + j) + nd] for j in range(2)] for i in range(2)]
        cols = [swap_bit((part[0][j], part[1][j]), 4, high_bit) for j in range(2)]
        for g1 in range(2):
            outs = swap_bit((cols[0][g1], cols[1][g1]), 1, low_bit)
            for g0 in range(2):
                send[:, block_of(2 * grp + g1), g0, :] = outs[g0]
    speed = m_ref[1]
    partial_sum = jnp.sum(jnp.sum(speed * speed, axis=1, keepdims=True), axis=0, keepdims=True)
    rate_own = jnp.full((1, 1), 0.25 * f_ref[0].astype(F32), F32)
    send[:, nvar, 0, :] = jnp.broadcast_to(rate_own, (nd, LANES))
    send[:, nvar, 1, :] = jnp.broadcast_to(partial_sum, (nd, LANES))

    recv[mh, ms] = send[me, 0 : nvar + 1]
    mrecv[ms] = send[me, nvar + 1 : nvar + 4]

    pl.semaphore_wait(barrier, nd - 1)

    def out_copy(kd, sd):
        d = kd * ns + sd
        return pltpu.make_async_remote_copy(
            src_ref=send.at[d, pl.ds(0, nvar + 1)],
            dst_ref=recv.at[mh, ms],
            send_sem=hs_sem.at[d],
            recv_sem=hr_sem.at[me],
            device_id=(kd, sd),
            device_id_type=MESH_ID,
        )

    def in_copy(kd, sd):
        d = kd * ns + sd
        return pltpu.make_async_remote_copy(
            src_ref=send.at[d, pl.ds(0, nvar + 1)],
            dst_ref=recv.at[kd, sd],
            send_sem=hs_sem.at[d],
            recv_sem=hr_sem.at[d],
            device_id=(kd, sd),
            device_id_type=MESH_ID,
        )

    def mean_copy(s, slot):
        return pltpu.make_async_remote_copy(
            src_ref=send.at[mh * ns + s, pl.ds(nvar + 1, 3)],
            dst_ref=mrecv.at[slot],
            send_sem=ms_sem.at[s],
            recv_sem=mr_sem.at[slot],
            device_id=(mh, s),
            device_id_type=MESH_ID,
        )

    for oh, os in far_first:
        out_copy(flip(mh, oh), flip(ms, os)).start()
        if oh == 1 and os == ns - 1:
            for o in range(ns - 1, 0, -1):
                mean_copy(flip(ms, o), ms).start()

    lane = lax.broadcasted_iota(jnp.int32, (nx, LANES), 1)
    cell = lax.broadcasted_iota(jnp.int32, (nx, LANES), 0)
    second = (lane >> 1) & 1
    is_real = second == 0

    def other(value):
        return jnp.where(is_real, pltpu.roll(value, LANES - 2, 1), pltpu.roll(value, 2, 1))

    def spread(value):
        turned = other(value)
        return jnp.where(is_real, value, turned), jnp.where(is_real, turned, value)

    for o in range(1, ns):
        peer = flip(ms, o)
        in_copy(mh, peer).wait_recv()
        mean_copy(peer, peer).wait_recv()
    packed = []
    for b in range(3):
        for s in range(ns):
            mean[b, cells * s : cells * s + cells, :] = mrecv[s, b]
        packed.append(mean[b])
    m4, wall = spread(packed[0])
    m0, m1 = spread(packed[1])
    m2, m3 = spread(packed[2])
    for a, value in enumerate((m0, m1, m2, m3, m4)):
        mean[a] = value
        mean0[a] = value
    total = recv[mh, 0, nvar, 1:2, :]
    for s in range(1, ns):
        total = total + recv[mh, s, nvar, 1:2, :]
    count = nx * tiles * LANES
    time_step = jnp.broadcast_to(0.9 / (1.0 + jnp.sqrt(total / count)), (nx, LANES))
    wall2 = 2.0 * wall
    z = (lane & 1) * nd + me
    radius = 0.5 + (z.astype(F32) + 0.5) / (2 * nd)
    inv_r = 1.0 / radius

    mp1 = jnp.where(cell < nx - 1, 1.0, 0.0).astype(F32)
    mm1 = jnp.where(cell > 0, 1.0, 0.0).astype(F32)
    mp2 = jnp.where(cell < nx - 2, 1.0, 0.0).astype(F32)
    mm2 = jnp.where(cell > 1, 1.0, 0.0).astype(F32)

    def xp(v, n):
        return pltpu.roll(v, nx - n, 0)

    def xm(v, n):
        return pltpu.roll(v, n, 0)

    def yp(v, n):
        return pltpu.roll(v, LANES - 4 * n, 1)

    def ym(v, n):
        return pltpu.roll(v, 4 * n, 1)

    def pieces(v, fwd, bwd):
        xp1, xm1 = xp(v, 1), xm(v, 1)
        yp1, ym1 = yp(v, 1), ym(v, 1)
        fourth = (
            mp2 * xp(v, 2) + mm2 * xm(v, 2) + 12.0 * v + yp(v, 2) + ym(v, 2)
            - 4.0 * (mp1 * xp1 + mm1 * xm1 + yp1 + ym1)
        )
        return fwd * xp1 - bwd * xm1, yp1 - ym1, fourth

    def mix(us, vs, a):
        flux = jx_ref[a, 0] * us[0]
        for b in range(1, nvar):
            flux = flux + jx_ref[a, b] * us[b]
        for b in range(nvar):
            flux = flux + jy_ref[a, b] * vs[b]
        return 0.5 * flux

    pairs = ((1, 1), (1, 2), (1, 3), (2, 2), (2, 3), (3, 3), (4, 1), (4, 2), (4, 3))

    zero = jnp.zeros((nx, LANES), F32)
    empty = (zero,) * len(pairs)

    def products(acc, hs):
        return tuple(s + hs[p] * hs[q] for s, (p, q) in zip(acc, pairs))

    def advance(k, hs, om, edges, step):
        om = jnp.where(is_real, om, -om)
        got = [pieces(h, *edges) for h in hs]
        us, vs = [g[0] for g in got], [g[1] for g in got]
        news = []
        for a in range(nvar):
            res = om * other(hs[a]) - mix(us, vs, a) - 0.05 * got[a][2] - wall2 * hs[a]
            news.append(first[k, a] + step * res)
        return news

    def edges_of(mc):
        return mp1 * xp(mc, 1), mm1 * xm(mc, 1)

    def gx(v):
        return 0.5 * (mp1 * xp(v, 1) - mm1 * xm(v, 1))

    def gy(v):
        return 0.5 * (yp(v, 1) - ym(v, 1))

    def advance_mean(acc, step):
        s = [0.5 * (v + other(v)) for v in acc]
        force = (
            zero,
            -gx(s[0]) - gy(s[1]),
            -gx(s[1]) - gy(s[3]) - 2.0 * s[4] * inv_r,
            -gx(s[2]) - gy(s[4]) + (s[3] - s[5]) * inv_r,
            -gx(s[6]) - gy(s[7]) - s[8] * inv_r,
        )
        got = [pieces(mean[a], mp1, mm1) for a in range(nvar)]
        us, vs = [g[0] for g in got], [g[1] for g in got]
        for a in range(nvar):
            res = force[a] - mix(us, vs, a) - 0.05 * got[a][2]
            mean[a] = mean0[a] + step * res

    edges = edges_of(mean[1])
    step = SECTION_RATES[0] * time_step

    def landed(k, accs):
        before, after = accs
        for s in range(ns):
            for a in range(nvar):
                first[k, a, cells * s : cells * s + cells, :] = recv[k, s, a]
        om = jnp.broadcast_to(recv[k, 0, nvar, 0:1, :], (nx, LANES))
        omega[k] = om
        hs = [first[k, a] for a in range(nvar)]
        news = advance(k, hs, om, edges, step)
        for a in range(nvar):
            state[k, a] = news[a]
        return products(before, hs), products(after, news)

    def arrive(o, accs):
        k = flip_by(mh, o)
        for os in range(ns):
            in_copy(k, flip(ms, os)).wait_recv()
        return landed(k, accs)

    before, acc = lax.fori_loop(1, nh, arrive, landed(mh, (empty, empty)))
    advance_mean(before, step)

    def section(i, acc):
        step = jnp.where(i == 1, SECTION_RATES[1], SECTION_RATES[2]).astype(F32) * time_step
        edges = edges_of(mean[1])

        def one(k, after):
            news = advance(k, [state[k, a] for a in range(nvar)], omega[k], edges, step)
            for a in range(nvar):
                state[k, a] = news[a]
            return products(after, news)

        after = lax.fori_loop(0, nh, one, empty, unroll=2)
        advance_mean(acc, step)
        return after

    acc = lax.fori_loop(1, 3, section, acc)

    step = SECTION_RATES[3] * time_step
    edges = edges_of(mean[1])
    advance_mean(acc, step)

    def join(even, odd):
        return jnp.where(is_real, even, odd)

    packs = (mean[4], join(mean[0], mean[1]), join(mean[2], mean[3]))

    def back_copy(k, s, slot):
        d = k * ns + s
        return pltpu.make_async_remote_copy(
            src_ref=back.at[k, s],
            dst_ref=home.at[slot],
            send_sem=bs_sem.at[d],
            recv_sem=br_sem.at[slot],
            device_id=(k, s),
            device_id_type=MESH_ID,
        )

    def finish(k):
        news = advance(k, [state[k, a] for a in range(nvar)], omega[k], edges, step)
        for s in range(ns):
            for a in range(nvar):
                back[k, s, a] = news[a][cells * s : cells * s + cells, :]
            for b in range(3):
                back[k, s, nvar + b] = packs[b][cells * s : cells * s + cells, :]

    def depart(o, _):
        k = flip_by(mh, nh - 1 - o)
        finish(k)
        for os in range(ns - 1, -1, -1):
            back_copy(k, flip(ms, os), me).start()
        return 0

    lax.fori_loop(0, nh - 1, depart, 0)
    finish(mh)
    for os in range(ns - 1, 0, -1):
        back_copy(mh, flip(ms, os), me).start()
    home[me] = back[mh, ms]

    def land_back(o, _):
        d = lax.rem(me + o, nd)
        back_copy(d // ns, lax.rem(d, ns), d).wait_recv()
        return 0

    lax.fori_loop(1, nd, land_back, 0)

    for grp in range(4):
        cols = []
        for g1 in range(2):
            cols.append(swap_bit([home[:, 2 * grp + g1, g0, :] for g0 in range(2)], 1, low_bit))
        part = [swap_bit((cols[0][j], cols[1][j]), 4, high_bit) for j in range(2)]
        mat = jnp.concatenate([part[j][i] for i in range(2) for j in range(2)], axis=0)
        turned = mat.T
        for t in range(tiles):
            rows[ROWS * grp : ROWS * grp + ROWS, LANES * t : LANES * t + LANES] = turned[
                ROWS * t : ROWS * t + ROWS
            ]

    def take(at):
        return rows[pl.ds(cells * at, cells), :]

    for a in range(nvar):
        for c in range(2):
            ho_ref[0, c, a] = take(2 * a + c)
    mo_ref[nvar - 1] = take(2 * nvar)
    for a in range(nvar - 1):
        mo_ref[a] = take(2 * nvar + 2 + a)

    def sent(o, _):
        d = lax.rem(me + o, nd)
        out_copy(d // ns, lax.rem(d, ns)).wait_send()
        back_copy(d // ns, lax.rem(d, ns), me).wait_send()
        return 0

    lax.fori_loop(1, nd, sent, 0)
    for o in range(1, ns):
        mean_copy(flip(ms, o), ms).wait_send()


def radial_shards(nh, ns, harmonics, mean_flow, freq_index, wall_mask, jacobian_x, jacobian_y):
    nvar, cells, planes = mean_flow.shape
    nd, nx = nh * ns, ns * cells
    vmem = pl.BlockSpec(memory_space=pltpu.VMEM)
    smem = pl.BlockSpec(memory_space=pltpu.SMEM)
    anywhere = pl.BlockSpec(memory_space=pl.ANY)
    dims = (nh, ns, nvar, cells, planes // LANES)
    field = (nx, LANES)
    piece = (cells, LANES)
    return pl.pallas_call(
        functools.partial(radial_kernel, dims),
        out_shape=(
            jax.ShapeDtypeStruct(mean_flow.shape, F32),
            jax.ShapeDtypeStruct(harmonics.shape, F32),
        ),
        in_specs=[anywhere, anywhere, smem, anywhere, smem, smem],
        out_specs=(vmem, vmem),
        scratch_shapes=[
            pltpu.VMEM(harmonics.shape, F32),
            pltpu.VMEM(mean_flow.shape, F32),
            pltpu.VMEM(wall_mask.shape, jnp.int32),
            pltpu.SemaphoreType.DMA((3,)),
            pltpu.VMEM((4 * ROWS, planes), F32),
            pltpu.VMEM((nd, nvar + 4, *piece), F32),
            pltpu.VMEM((nh, ns, nvar + 1, *piece), F32),
            pltpu.VMEM((ns, 3, *piece), F32),
            pltpu.VMEM((nh, nvar, *field), F32),
            pltpu.VMEM((nh, nvar, *field), F32),
            pltpu.VMEM((nh, *field), F32),
            pltpu.VMEM((nvar, *field), F32),
            pltpu.VMEM((nvar, *field), F32),
            pltpu.VMEM((nh, ns, nvar + 3, *piece), F32),
            pltpu.VMEM((nd, nvar + 3, *piece), F32),
            pltpu.SemaphoreType.DMA((nd,)),
            pltpu.SemaphoreType.DMA((nd,)),
            pltpu.SemaphoreType.DMA((ns,)),
            pltpu.SemaphoreType.DMA((ns,)),
            pltpu.SemaphoreType.DMA((nd,)),
            pltpu.SemaphoreType.DMA((nd,)),
        ],
        compiler_params=pltpu.CompilerParams(collective_id=0, has_side_effects=True),
    )(harmonics, mean_flow, freq_index, wall_mask, jacobian_x, jacobian_y)


def fits_radial(nh, ns, harmonics, mean_flow):
    owned, parts, nvar, cells, planes = harmonics.shape
    return (
        NZ == 2 * nh * ns
        and LANES == 2 * NZ
        and (owned, parts, nvar, cells) == (1, 2, 5, 2)
        and ns * cells == ROWS
        and planes == 16 * LANES
    )


def either(nh, ns, harmonics, mean_flow, *rest):
    if fits_radial(nh, ns, harmonics, mean_flow):
        return radial_shards(nh, ns, harmonics, mean_flow, *rest)
    return shards(harmonics, mean_flow, *rest)


def solution(mesh):
    placed = (
        P("harm", None, None, "slab", None),
        P(None, "slab", None),
        P("harm"),
        P("slab", None),
        P(),
        P(),
    )
    return jax.shard_map(
        functools.partial(either, mesh.shape["harm"], mesh.shape["slab"]),
        mesh=mesh,
        in_specs=placed,
        out_specs=(P(None, "slab", None), P("harm", None, None, "slab", None)),
        check_vma=False,
    )
```

```python
import functools

import jax
import jax.numpy as jnp
from jax import lax
from jax.experimental import pallas as pl
from jax.experimental.pallas import tpu as pltpu
from jax.sharding import PartitionSpec as P

NZ = 64


EPS_FOURTH = 0.05
COURANT = 0.9
OMEGA_BASE = 0.25
WALL_RATE = 2.0
HUB_RADIUS = 0.5
SECTION_RATES = (0.25, 1.0 / 3.0, 0.5, 1.0)
STRESS_PAIRS = ((1, 1), (1, 2), (1, 3), (2, 2), (2, 3), (3, 3), (4, 1), (4, 2), (4, 3))


def with_halo(cells, sides, width):
    for axis, dim in sides:
        count = lax.axis_size(axis)
        ends = count - 1
        head = lax.slice_in_dim(cells, 0, width, axis=dim)
        tail = lax.slice_in_dim(cells, cells.shape[dim] - width, cells.shape[dim], axis=dim)
        cells = jnp.concatenate(
            [
                lax.ppermute(tail, axis, [(i, (i + 1) % count) for i in range(ends)]),
                cells,
                lax.ppermute(head, axis, [((i + 1) % count, i) for i in range(ends)]),
            ],
            axis=dim,
        )
    return cells


def apply_matrix(matrix, values):
    return jnp.einsum("ab,...bxp->...axp", matrix, values, precision=lax.Precision.HIGHEST)


def diff_across(values):
    return (jnp.roll(values, -NZ, axis=-1) - jnp.roll(values, NZ, axis=-1)) * 0.5


def fourth_across(values):
    return (
        jnp.roll(values, -2 * NZ, axis=-1)
        - 4.0 * jnp.roll(values, -NZ, axis=-1)
        + 6.0 * values
        - 4.0 * jnp.roll(values, NZ, axis=-1)
        + jnp.roll(values, 2 * NZ, axis=-1)
    )


def diff_along(padded):
    return (padded[..., 3:-1, :] - padded[..., 1:-3, :]) * 0.5


def fourth_along(padded):
    return (
        padded[..., 4:, :]
        - 4.0 * padded[..., 3:-1, :]
        + 6.0 * padded[..., 2:-2, :]
        - 4.0 * padded[..., 1:-3, :]
        + padded[..., :-4, :]
    )


def harmonic_residual(harm_pad, momentum_pad, omegas, wall_cells, jac_x, jac_y):
    center = harm_pad[..., 2:-2, :]
    flux_x = apply_matrix(jac_x, harm_pad * momentum_pad)
    flux_y = apply_matrix(jac_y, center)
    rotation = jnp.stack([center[..., 1, :, :, :], -center[..., 0, :, :, :]], axis=-4) * omegas
    return (
        rotation
        - diff_along(flux_x)
        - diff_across(flux_y)
        - EPS_FOURTH * (fourth_along(harm_pad) + fourth_across(center))
        - WALL_RATE * wall_cells * center
    )


def stresses(values):
    fields = []
    for first, second in STRESS_PAIRS:
        product = values[..., first, :, :] * values[..., second, :, :]
        fields.append(0.5 * jnp.sum(product, axis=tuple(range(product.ndim - 2))))
    return jnp.stack(fields, axis=0)


def forcing(stress_pad, radius):
    center = stress_pad[:, 1:-1, :]
    grad_x = (stress_pad[:, 2:, :] - stress_pad[:, :-2, :]) * 0.5
    grad_y = diff_across(center)
    first = -grad_x[0] - grad_y[1]
    second = -grad_x[1] - grad_y[3] - 2.0 * center[4] / radius
    third = -grad_x[2] - grad_y[4] + (center[3] - center[5]) / radius
    fourth = -grad_x[6] - grad_y[7] - center[8] / radius
    return jnp.stack([first, second, third, fourth], axis=0)


def mean_residual(mean_pad, forcing_terms, jac_x, jac_y):
    center = mean_pad[:, 2:-2, :]
    residual = (
        -diff_along(apply_matrix(jac_x, mean_pad))
        - diff_across(apply_matrix(jac_y, center))
        - EPS_FOURTH * (fourth_along(mean_pad) + fourth_across(center))
    )
    zeros_row = jnp.zeros_like(forcing_terms[:1])
    return residual + jnp.concatenate([zeros_row, forcing_terms], axis=0)


def shards(harmonics, mean_flow, freq_index, wall_mask, jacobian_x, jacobian_y):
    owned = harmonics.shape[0]
    slab_cells = mean_flow.shape[1]
    plane_count = mean_flow.shape[2]
    radius = HUB_RADIUS + ((jnp.arange(plane_count) % NZ).astype(jnp.float32) + 0.5) / NZ
    wall_cells = wall_mask.astype(jnp.float32)
    omegas = (OMEGA_BASE * freq_index.astype(jnp.float32)).reshape(owned, 1, 1, 1, 1)
    speed_total = lax.psum(jnp.sum(mean_flow[1] * mean_flow[1]), "slab")
    cell_count = slab_cells * lax.axis_size("slab") * plane_count
    time_step = COURANT / (1.0 + jnp.sqrt(speed_total / cell_count))
    harm_now, mean_now = (harmonics, mean_flow)
    for section_rate in SECTION_RATES:
        stacked = jnp.concatenate(
            [harm_now.reshape(owned * 2, 5, slab_cells, plane_count), mean_now[None]], axis=0
        )
        padded = with_halo(stacked, (("slab", 2),), 2)
        harm_pad = padded[: 2 * owned].reshape(owned, 2, 5, slab_cells + 4, plane_count)
        mean_pad = padded[2 * owned]
        harm_res = harmonic_residual(
            harm_pad, mean_pad[1], omegas, wall_cells, jacobian_x, jacobian_y
        )
        partial_terms = forcing(stresses(harm_pad[..., 1:-1, :]), radius)
        forcing_terms = lax.psum(partial_terms, "harm")
        mean_res = mean_residual(mean_pad, forcing_terms, jacobian_x, jacobian_y)
        harm_now = harmonics + section_rate * time_step * harm_res
        mean_now = mean_flow + section_rate * time_step * mean_res
    return (mean_now, harm_now)


MESH_ID = pl.DeviceIdType.MESH
LANES = 128
ROWS = 8
F32 = jnp.float32


def swap_bit(pair, stride, bit):
    low, high = pair
    return (
        jnp.where(bit == 0, low, pltpu.roll(high, stride, 1)),
        jnp.where(bit == 0, pltpu.roll(low, LANES - stride, 1), high),
    )


def radial_kernel(
    dims, h_any, m_any, f_ref, w_any, jx_ref, jy_ref, mo_ref, ho_ref,
    h_ref, m_ref, w_ref, in_sem, rows, send, relay, recv, mrecv, state, first, omega, mean, mean0, back, home,
    hs_sem, hr_sem, zs_sem, zr_sem, ms_sem, mr_sem, bs_sem, br_sem,
):
    nh, ns, nvar, cells, tiles = dims
    nd = nh * ns
    mh, ms = lax.axis_index("harm"), lax.axis_index("slab")
    me = mh * ns + ms
    nx = ns * cells
    nz, nc = nh // 2, 2 * ns
    mz, mx = mh // 2, lax.rem(mh, 2)
    mc = mx * ns + ms

    barrier = pltpu.get_barrier_semaphore()

    def flip(index, bits):
        out = index
        weight = 1
        while weight <= bits:
            if bits & weight:
                out = out + weight * (1 - 2 * lax.rem(index // weight, 2))
            weight *= 2
        return out

    def flip_by(index, bits):
        out = index
        weight = 1
        while weight < nh:
            out = out + lax.rem(bits // weight, 2) * weight * (1 - 2 * lax.rem(index // weight, 2))
            weight *= 2
        return out

    near = [(ox, os) for os in range(ns - 1, -1, -1) for ox in (1, 0) if ox or os]
    lines = range(nz - 1, 0, -1)

    for z in lines:
        pl.semaphore_signal(
            barrier, inc=1, device_id=(2 * flip(mz, z) + mx, ms), device_id_type=MESH_ID
        )
    for ox, os in near:
        pl.semaphore_signal(
            barrier, inc=1, device_id=(2 * mz + flip(mx, ox), flip(ms, os)), device_id_type=MESH_ID
        )
    loads = [
        pltpu.make_async_copy(src, dst, in_sem.at[i])
        for i, (src, dst) in enumerate(((h_any, h_ref), (m_any, m_ref), (w_any, w_ref)))
    ]
    for load in loads:
        load.start()
    for load in loads:
        load.wait()

    lane_all = lax.broadcasted_iota(jnp.int32, (nd, LANES), 1)
    low_bit = lane_all & 1
    high_bit = (lane_all >> 2) & 1

    def place(at, value):
        rows[pl.ds(cells * at, cells), :] = value

    for a in range(nvar):
        for c in range(2):
            place(2 * a + c, h_ref[0, c, a])
    place(2 * nvar, m_ref[nvar - 1])
    place(2 * nvar + 1, w_ref[...].astype(F32))
    for a in range(nvar - 1):
        place(2 * nvar + 2 + a, m_ref[a])

    def block_of(g):
        return g if g < nvar else g + 1

    for grp in range(4):
        mat = jnp.concatenate(
            [rows[ROWS * grp : ROWS * grp + ROWS, LANES * t : LANES * t + LANES] for t in range(tiles)],
            axis=0,
        )
        turned = mat.T
        part = [[turned[nd * (2 * i + j) : nd * (2 * i + j) + nd] for j in range(2)] for i in range(2)]
        cols = [swap_bit((part[0][j], part[1][j]), 4, high_bit) for j in range(2)]
        for g1 in range(2):
            outs = swap_bit((cols[0][g1], cols[1][g1]), 1, low_bit)
            for g0 in range(2):
                for z in range(nz):
                    send[z, :, block_of(2 * grp + g1), g0, :] = outs[g0][nc * z : nc * z + nc]
    speed = m_ref[1]
    partial_sum = jnp.sum(jnp.sum(speed * speed, axis=1, keepdims=True), axis=0, keepdims=True)
    rate_own = jnp.full((1, 1), 0.25 * f_ref[0].astype(F32), F32)
    send[:, :, nvar, 0, :] = jnp.broadcast_to(rate_own, (nz, nc, LANES))
    send[:, :, nvar, 1, :] = jnp.broadcast_to(partial_sum, (nz, nc, LANES))

    for z in range(nz):
        relay[z, mc] = send[z, mc, 0 : nvar + 1]
    mrecv[ms] = send[mz, mc, nvar + 1 : nvar + 4]

    pl.semaphore_wait(barrier, nz - 1 + nc - 1)

    def near_copy(px, ps, slot):
        pc = px * ns + ps
        return pltpu.make_async_remote_copy(
            src_ref=send.at[:, pc, pl.ds(0, nvar + 1)],
            dst_ref=relay.at[:, slot],
            send_sem=hs_sem.at[pc],
            recv_sem=hr_sem.at[slot],
            device_id=(2 * mz + px, ps),
            device_id_type=MESH_ID,
        )

    def line_copy(pz, slot):
        return pltpu.make_async_remote_copy(
            src_ref=relay.at[pz],
            dst_ref=recv.at[slot],
            send_sem=zs_sem.at[pz],
            recv_sem=zr_sem.at[slot],
            device_id=(2 * pz + mx, ms),
            device_id_type=MESH_ID,
        )

    def mean_copy(s, slot):
        return pltpu.make_async_remote_copy(
            src_ref=send.at[mz, mx * ns + s, pl.ds(nvar + 1, 3)],
            dst_ref=mrecv.at[slot],
            send_sem=ms_sem.at[s],
            recv_sem=mr_sem.at[slot],
            device_id=(mh, s),
            device_id_type=MESH_ID,
        )

    for ox, os in near:
        near_copy(flip(mx, ox), flip(ms, os), mc).start()
    for o in range(ns - 1, 0, -1):
        mean_copy(flip(ms, o), ms).start()
    for ox, os in near:
        px, ps = flip(mx, ox), flip(ms, os)
        near_copy(px, ps, px * ns + ps).wait_recv()
    for z in lines:
        line_copy(flip(mz, z), mz).start()
    recv[mz] = relay[mz]

    lane = lax.broadcasted_iota(jnp.int32, (nx, LANES), 1)
    cell = lax.broadcasted_iota(jnp.int32, (nx, LANES), 0)
    second = (lane >> 1) & 1
    is_real = second == 0

    def other(value):
        return jnp.where(is_real, pltpu.roll(value, LANES - 2, 1), pltpu.roll(value, 2, 1))

    def spread(value):
        turned = other(value)
        return jnp.where(is_real, value, turned), jnp.where(is_real, turned, value)

    for o in range(1, ns):
        peer = flip(ms, o)
        mean_copy(peer, peer).wait_recv()
    packed = []
    for b in range(3):
        for s in range(ns):
            mean[b, cells * s : cells * s + cells, :] = mrecv[s, b]
        packed.append(mean[b])
    m4, wall = spread(packed[0])
    m0, m1 = spread(packed[1])
    m2, m3 = spread(packed[2])
    for a, value in enumerate((m0, m1, m2, m3, m4)):
        mean[a] = value
        mean0[a] = value
    total = recv[mz, mx * ns, nvar, 1:2, :]
    for s in range(1, ns):
        total = total + recv[mz, mx * ns + s, nvar, 1:2, :]
    count = nx * tiles * LANES
    time_step = jnp.broadcast_to(0.9 / (1.0 + jnp.sqrt(total / count)), (nx, LANES))
    wall2 = 2.0 * wall
    z = (lane & 1) * nd + me
    radius = 0.5 + (z.astype(F32) + 0.5) / (2 * nd)
    inv_r = 1.0 / radius

    mp1 = jnp.where(cell < nx - 1, 1.0, 0.0).astype(F32)
    mm1 = jnp.where(cell > 0, 1.0, 0.0).astype(F32)
    mp2 = jnp.where(cell < nx - 2, 1.0, 0.0).astype(F32)
    mm2 = jnp.where(cell > 1, 1.0, 0.0).astype(F32)

    def xp(v, n):
        return pltpu.roll(v, nx - n, 0)

    def xm(v, n):
        return pltpu.roll(v, n, 0)

    def yp(v, n):
        return pltpu.roll(v, LANES - 4 * n, 1)

    def ym(v, n):
        return pltpu.roll(v, 4 * n, 1)

    def pieces(v, fwd, bwd):
        xp1, xm1 = xp(v, 1), xm(v, 1)
        yp1, ym1 = yp(v, 1), ym(v, 1)
        fourth = (
            mp2 * xp(v, 2) + mm2 * xm(v, 2) + 12.0 * v + yp(v, 2) + ym(v, 2)
            - 4.0 * (mp1 * xp1 + mm1 * xm1 + yp1 + ym1)
        )
        return fwd * xp1 - bwd * xm1, yp1 - ym1, fourth

    def mix(us, vs, a):
        flux = jx_ref[a, 0] * us[0]
        for b in range(1, nvar):
            flux = flux + jx_ref[a, b] * us[b]
        for b in range(nvar):
            flux = flux + jy_ref[a, b] * vs[b]
        return 0.5 * flux

    pairs = ((1, 1), (1, 2), (1, 3), (2, 2), (2, 3), (3, 3), (4, 1), (4, 2), (4, 3))

    zero = jnp.zeros((nx, LANES), F32)
    empty = (zero,) * len(pairs)

    def products(acc, hs):
        return tuple(s + hs[p] * hs[q] for s, (p, q) in zip(acc, pairs))

    def advance(k, hs, om, edges, step):
        om = jnp.where(is_real, om, -om)
        got = [pieces(h, *edges) for h in hs]
        us, vs = [g[0] for g in got], [g[1] for g in got]
        news = []
        for a in range(nvar):
            res = om * other(hs[a]) - mix(us, vs, a) - 0.05 * got[a][2] - wall2 * hs[a]
            news.append(first[k, a] + step * res)
        return news

    def edges_of(mc):
        return mp1 * xp(mc, 1), mm1 * xm(mc, 1)

    def gx(v):
        return 0.5 * (mp1 * xp(v, 1) - mm1 * xm(v, 1))

    def gy(v):
        return 0.5 * (yp(v, 1) - ym(v, 1))

    def advance_mean(acc, step):
        s = [0.5 * (v + other(v)) for v in acc]
        force = (
            zero,
            -gx(s[0]) - gy(s[1]),
            -gx(s[1]) - gy(s[3]) - 2.0 * s[4] * inv_r,
            -gx(s[2]) - gy(s[4]) + (s[3] - s[5]) * inv_r,
            -gx(s[6]) - gy(s[7]) - s[8] * inv_r,
        )
        got = [pieces(mean[a], mp1, mm1) for a in range(nvar)]
        us, vs = [g[0] for g in got], [g[1] for g in got]
        for a in range(nvar):
            res = force[a] - mix(us, vs, a) - 0.05 * got[a][2]
            mean[a] = mean0[a] + step * res

    edges = edges_of(mean[1])
    step = SECTION_RATES[0] * time_step

    def landed(z, x, accs):
        k = 2 * z + x
        before, after = accs
        for s in range(ns):
            for a in range(nvar):
                first[k, a, cells * s : cells * s + cells, :] = recv[z, x * ns + s, a]
        om = jnp.broadcast_to(recv[z, x * ns, nvar, 0:1, :], (nx, LANES))
        omega[k] = om
        hs = [first[k, a] for a in range(nvar)]
        news = advance(k, hs, om, edges, step)
        for a in range(nvar):
            state[k, a] = news[a]
        return products(before, hs), products(after, news)

    accs = (empty, empty)
    for oz in range(nz):
        z = flip(mz, oz)
        if oz:
            line_copy(z, z).wait_recv()
        accs = lax.fori_loop(0, 2, functools.partial(lambda z, x, accs: landed(z, x, accs), z), accs)
    before, acc = accs
    advance_mean(before, step)

    def section(i, acc):
        step = jnp.where(i == 1, SECTION_RATES[1], SECTION_RATES[2]).astype(F32) * time_step
        edges = edges_of(mean[1])

        def one(k, after):
            news = advance(k, [state[k, a] for a in range(nvar)], omega[k], edges, step)
            for a in range(nvar):
                state[k, a] = news[a]
            return products(after, news)

        after = lax.fori_loop(0, nh, one, empty, unroll=2)
        advance_mean(acc, step)
        return after

    acc = lax.fori_loop(1, 3, section, acc)

    step = SECTION_RATES[3] * time_step
    edges = edges_of(mean[1])
    advance_mean(acc, step)

    def join(even, odd):
        return jnp.where(is_real, even, odd)

    packs = (mean[4], join(mean[0], mean[1]), join(mean[2], mean[3]))

    def back_copy(k, s, slot):
        d = k * ns + s
        return pltpu.make_async_remote_copy(
            src_ref=back.at[k, s],
            dst_ref=home.at[slot],
            send_sem=bs_sem.at[d],
            recv_sem=br_sem.at[slot],
            device_id=(k, s),
            device_id_type=MESH_ID,
        )

    def finish(k):
        news = advance(k, [state[k, a] for a in range(nvar)], omega[k], edges, step)
        for s in range(ns):
            for a in range(nvar):
                back[k, s, a] = news[a][cells * s : cells * s + cells, :]
            for b in range(3):
                back[k, s, nvar + b] = packs[b][cells * s : cells * s + cells, :]

    def depart(o, _):
        k = flip_by(mh, nh - 1 - o)
        finish(k)
        for os in range(ns - 1, -1, -1):
            back_copy(k, flip(ms, os), me).start()
        return 0

    lax.fori_loop(0, nh - 1, depart, 0)
    finish(mh)
    for os in range(ns - 1, 0, -1):
        back_copy(mh, flip(ms, os), me).start()
    home[me] = back[mh, ms]

    def land_back(o, _):
        d = lax.rem(me + o, nd)
        back_copy(d // ns, lax.rem(d, ns), d).wait_recv()
        return 0

    lax.fori_loop(1, nd, land_back, 0)

    for grp in range(4):
        cols = []
        for g1 in range(2):
            cols.append(swap_bit([home[:, 2 * grp + g1, g0, :] for g0 in range(2)], 1, low_bit))
        part = [swap_bit((cols[0][j], cols[1][j]), 4, high_bit) for j in range(2)]
        mat = jnp.concatenate([part[j][i] for i in range(2) for j in range(2)], axis=0)
        turned = mat.T
        for t in range(tiles):
            rows[ROWS * grp : ROWS * grp + ROWS, LANES * t : LANES * t + LANES] = turned[
                ROWS * t : ROWS * t + ROWS
            ]

    def take(at):
        return rows[pl.ds(cells * at, cells), :]

    for a in range(nvar):
        for c in range(2):
            ho_ref[0, c, a] = take(2 * a + c)
    mo_ref[nvar - 1] = take(2 * nvar)
    for a in range(nvar - 1):
        mo_ref[a] = take(2 * nvar + 2 + a)

    def sent(o, _):
        d = lax.rem(me + o, nd)
        back_copy(d // ns, lax.rem(d, ns), me).wait_send()
        return 0

    lax.fori_loop(1, nd, sent, 0)
    for o in range(1, ns):
        mean_copy(flip(ms, o), ms).wait_send()
    for ox, os in near:
        near_copy(flip(mx, ox), flip(ms, os), mc).wait_send()
    for z in lines:
        line_copy(flip(mz, z), mz).wait_send()


def radial_shards(nh, ns, harmonics, mean_flow, freq_index, wall_mask, jacobian_x, jacobian_y):
    nvar, cells, planes = mean_flow.shape
    nd, nx = nh * ns, ns * cells
    vmem = pl.BlockSpec(memory_space=pltpu.VMEM)
    smem = pl.BlockSpec(memory_space=pltpu.SMEM)
    anywhere = pl.BlockSpec(memory_space=pl.ANY)
    dims = (nh, ns, nvar, cells, planes // LANES)
    field = (nx, LANES)
    piece = (cells, LANES)
    return pl.pallas_call(
        functools.partial(radial_kernel, dims),
        out_shape=(
            jax.ShapeDtypeStruct(mean_flow.shape, F32),
            jax.ShapeDtypeStruct(harmonics.shape, F32),
        ),
        in_specs=[anywhere, anywhere, smem, anywhere, smem, smem],
        out_specs=(vmem, vmem),
        scratch_shapes=[
            pltpu.VMEM(harmonics.shape, F32),
            pltpu.VMEM(mean_flow.shape, F32),
            pltpu.VMEM(wall_mask.shape, jnp.int32),
            pltpu.SemaphoreType.DMA((3,)),
            pltpu.VMEM((4 * ROWS, planes), F32),
            pltpu.VMEM((nh // 2, 2 * ns, nvar + 4, *piece), F32),
            pltpu.VMEM((nh // 2, 2 * ns, nvar + 1, *piece), F32),
            pltpu.VMEM((nh // 2, 2 * ns, nvar + 1, *piece), F32),
            pltpu.VMEM((ns, 3, *piece), F32),
            pltpu.VMEM((nh, nvar, *field), F32),
            pltpu.VMEM((nh, nvar, *field), F32),
            pltpu.VMEM((nh, *field), F32),
            pltpu.VMEM((nvar, *field), F32),
            pltpu.VMEM((nvar, *field), F32),
            pltpu.VMEM((nh, ns, nvar + 3, *piece), F32),
            pltpu.VMEM((nd, nvar + 3, *piece), F32),
            pltpu.SemaphoreType.DMA((2 * ns,)),
            pltpu.SemaphoreType.DMA((2 * ns,)),
            pltpu.SemaphoreType.DMA((nh // 2,)),
            pltpu.SemaphoreType.DMA((nh // 2,)),
            pltpu.SemaphoreType.DMA((ns,)),
            pltpu.SemaphoreType.DMA((ns,)),
            pltpu.SemaphoreType.DMA((nd,)),
            pltpu.SemaphoreType.DMA((nd,)),
        ],
        compiler_params=pltpu.CompilerParams(collective_id=0, has_side_effects=True),
    )(harmonics, mean_flow, freq_index, wall_mask, jacobian_x, jacobian_y)


def fits_radial(nh, ns, harmonics, mean_flow):
    owned, parts, nvar, cells, planes = harmonics.shape
    return (
        NZ == 2 * nh * ns
        and LANES == 2 * NZ
        and (owned, parts, nvar, cells) == (1, 2, 5, 2)
        and ns * cells == ROWS
        and planes == 16 * LANES
    )


def either(nh, ns, harmonics, mean_flow, *rest):
    if fits_radial(nh, ns, harmonics, mean_flow):
        return radial_shards(nh, ns, harmonics, mean_flow, *rest)
    return shards(harmonics, mean_flow, *rest)


def solution(mesh):
    placed = (
        P("harm", None, None, "slab", None),
        P(None, "slab", None),
        P("harm"),
        P("slab", None),
        P(),
        P(),
    )
    return jax.shard_map(
        functools.partial(either, mesh.shape["harm"], mesh.shape["slab"]),
        mesh=mesh,
        in_specs=placed,
        out_specs=(P(None, "slab", None), P("harm", None, None, "slab", None)),
        check_vma=False,
    )
```

```python
import functools

import jax
import jax.numpy as jnp
from jax import lax
from jax.experimental import pallas as pl
from jax.experimental.pallas import tpu as pltpu
from jax.sharding import PartitionSpec as P

NZ = 64


EPS_FOURTH = 0.05
COURANT = 0.9
OMEGA_BASE = 0.25
WALL_RATE = 2.0
HUB_RADIUS = 0.5
SECTION_RATES = (0.25, 1.0 / 3.0, 0.5, 1.0)
STRESS_PAIRS = ((1, 1), (1, 2), (1, 3), (2, 2), (2, 3), (3, 3), (4, 1), (4, 2), (4, 3))


def with_halo(cells, sides, width):
    for axis, dim in sides:
        count = lax.axis_size(axis)
        ends = count - 1
        head = lax.slice_in_dim(cells, 0, width, axis=dim)
        tail = lax.slice_in_dim(cells, cells.shape[dim] - width, cells.shape[dim], axis=dim)
        cells = jnp.concatenate(
            [
                lax.ppermute(tail, axis, [(i, (i + 1) % count) for i in range(ends)]),
                cells,
                lax.ppermute(head, axis, [((i + 1) % count, i) for i in range(ends)]),
            ],
            axis=dim,
        )
    return cells


def apply_matrix(matrix, values):
    return jnp.einsum("ab,...bxp->...axp", matrix, values, precision=lax.Precision.HIGHEST)


def diff_across(values):
    return (jnp.roll(values, -NZ, axis=-1) - jnp.roll(values, NZ, axis=-1)) * 0.5


def fourth_across(values):
    return (
        jnp.roll(values, -2 * NZ, axis=-1)
        - 4.0 * jnp.roll(values, -NZ, axis=-1)
        + 6.0 * values
        - 4.0 * jnp.roll(values, NZ, axis=-1)
        + jnp.roll(values, 2 * NZ, axis=-1)
    )


def diff_along(padded):
    return (padded[..., 3:-1, :] - padded[..., 1:-3, :]) * 0.5


def fourth_along(padded):
    return (
        padded[..., 4:, :]
        - 4.0 * padded[..., 3:-1, :]
        + 6.0 * padded[..., 2:-2, :]
        - 4.0 * padded[..., 1:-3, :]
        + padded[..., :-4, :]
    )


def harmonic_residual(harm_pad, momentum_pad, omegas, wall_cells, jac_x, jac_y):
    center = harm_pad[..., 2:-2, :]
    flux_x = apply_matrix(jac_x, harm_pad * momentum_pad)
    flux_y = apply_matrix(jac_y, center)
    rotation = jnp.stack([center[..., 1, :, :, :], -center[..., 0, :, :, :]], axis=-4) * omegas
    return (
        rotation
        - diff_along(flux_x)
        - diff_across(flux_y)
        - EPS_FOURTH * (fourth_along(harm_pad) + fourth_across(center))
        - WALL_RATE * wall_cells * center
    )


def stresses(values):
    fields = []
    for first, second in STRESS_PAIRS:
        product = values[..., first, :, :] * values[..., second, :, :]
        fields.append(0.5 * jnp.sum(product, axis=tuple(range(product.ndim - 2))))
    return jnp.stack(fields, axis=0)


def forcing(stress_pad, radius):
    center = stress_pad[:, 1:-1, :]
    grad_x = (stress_pad[:, 2:, :] - stress_pad[:, :-2, :]) * 0.5
    grad_y = diff_across(center)
    first = -grad_x[0] - grad_y[1]
    second = -grad_x[1] - grad_y[3] - 2.0 * center[4] / radius
    third = -grad_x[2] - grad_y[4] + (center[3] - center[5]) / radius
    fourth = -grad_x[6] - grad_y[7] - center[8] / radius
    return jnp.stack([first, second, third, fourth], axis=0)


def mean_residual(mean_pad, forcing_terms, jac_x, jac_y):
    center = mean_pad[:, 2:-2, :]
    residual = (
        -diff_along(apply_matrix(jac_x, mean_pad))
        - diff_across(apply_matrix(jac_y, center))
        - EPS_FOURTH * (fourth_along(mean_pad) + fourth_across(center))
    )
    zeros_row = jnp.zeros_like(forcing_terms[:1])
    return residual + jnp.concatenate([zeros_row, forcing_terms], axis=0)


def shards(harmonics, mean_flow, freq_index, wall_mask, jacobian_x, jacobian_y):
    owned = harmonics.shape[0]
    slab_cells = mean_flow.shape[1]
    plane_count = mean_flow.shape[2]
    radius = HUB_RADIUS + ((jnp.arange(plane_count) % NZ).astype(jnp.float32) + 0.5) / NZ
    wall_cells = wall_mask.astype(jnp.float32)
    omegas = (OMEGA_BASE * freq_index.astype(jnp.float32)).reshape(owned, 1, 1, 1, 1)
    speed_total = lax.psum(jnp.sum(mean_flow[1] * mean_flow[1]), "slab")
    cell_count = slab_cells * lax.axis_size("slab") * plane_count
    time_step = COURANT / (1.0 + jnp.sqrt(speed_total / cell_count))
    harm_now, mean_now = (harmonics, mean_flow)
    for section_rate in SECTION_RATES:
        stacked = jnp.concatenate(
            [harm_now.reshape(owned * 2, 5, slab_cells, plane_count), mean_now[None]], axis=0
        )
        padded = with_halo(stacked, (("slab", 2),), 2)
        harm_pad = padded[: 2 * owned].reshape(owned, 2, 5, slab_cells + 4, plane_count)
        mean_pad = padded[2 * owned]
        harm_res = harmonic_residual(
            harm_pad, mean_pad[1], omegas, wall_cells, jacobian_x, jacobian_y
        )
        partial_terms = forcing(stresses(harm_pad[..., 1:-1, :]), radius)
        forcing_terms = lax.psum(partial_terms, "harm")
        mean_res = mean_residual(mean_pad, forcing_terms, jacobian_x, jacobian_y)
        harm_now = harmonics + section_rate * time_step * harm_res
        mean_now = mean_flow + section_rate * time_step * mean_res
    return (mean_now, harm_now)


MESH_ID = pl.DeviceIdType.MESH
LANES = 128
ROWS = 8
F32 = jnp.float32


def swap_bit(pair, stride, bit):
    low, high = pair
    return (
        jnp.where(bit == 0, low, pltpu.roll(high, stride, 1)),
        jnp.where(bit == 0, pltpu.roll(low, LANES - stride, 1), high),
    )


def radial_kernel(
    dims, h_any, m_any, f_ref, w_any, jx_ref, jy_ref, home,
    h_ref, m_ref, w_ref, in_sem, rows, send, recv, mrecv, state, first, omega, mean, mean0, back, own_sem,
    hs_sem, hr_sem, ms_sem, mr_sem, bs_sem, br_sem,
):
    nh, ns, nvar, cells, tiles = dims
    nd = nh * ns
    mh, ms = lax.axis_index("harm"), lax.axis_index("slab")
    me = mh * ns + ms
    nx = ns * cells

    barrier = pltpu.get_barrier_semaphore()

    def flip(index, bits):
        out = index
        weight = 1
        while weight <= bits:
            if bits & weight:
                out = out + weight * (1 - 2 * lax.rem(index // weight, 2))
            weight *= 2
        return out

    def flip_by(index, bits):
        out = index
        weight = 1
        while weight < nh:
            out = out + lax.rem(bits // weight, 2) * weight * (1 - 2 * lax.rem(index // weight, 2))
            weight *= 2
        return out

    def reach(offset):
        oh, os = offset
        return min(oh >> 1, 2) + (oh & 1) + (os >> 1) + 0.3 * (os & 1)

    far_first = sorted(
        [(oh, os) for oh in range(nh) for os in range(ns) if oh or os], key=reach, reverse=True
    )
    for oh, os in far_first:
        pl.semaphore_signal(
            barrier, inc=1, device_id=(flip(mh, oh), flip(ms, os)), device_id_type=MESH_ID
        )
    loads = [
        pltpu.make_async_copy(src, dst, in_sem.at[i])
        for i, (src, dst) in enumerate(((h_any, h_ref), (m_any, m_ref), (w_any, w_ref)))
    ]
    for load in loads:
        load.start()
    for load in loads:
        load.wait()

    lane_all = lax.broadcasted_iota(jnp.int32, (nd, LANES), 1)
    low_bit = lane_all & 1
    high_bit = (lane_all >> 2) & 1

    def place(at, value):
        rows[pl.ds(cells * at, cells), :] = value

    for a in range(nvar):
        for c in range(2):
            place(2 * a + c, h_ref[0, c, a])
    place(2 * nvar, m_ref[nvar - 1])
    place(2 * nvar + 1, w_ref[...].astype(F32))
    for a in range(nvar - 1):
        place(2 * nvar + 2 + a, m_ref[a])

    def block_of(g):
        return g if g < nvar else g + 1

    for grp in range(4):
        mat = jnp.concatenate(
            [rows[ROWS * grp : ROWS * grp + ROWS, LANES * t : LANES * t + LANES] for t in range(tiles)],
            axis=0,
        )
        turned = mat.T
        part = [[turned[nd * (2 * i + j) : nd * (2 * i + j) + nd] for j in range(2)] for i in range(2)]
        cols = [swap_bit((part[0][j], part[1][j]), 4, high_bit) for j in range(2)]
        for g1 in range(2):
            outs = swap_bit((cols[0][g1], cols[1][g1]), 1, low_bit)
            for g0 in range(2):
                send[:, block_of(2 * grp + g1), g0, :] = outs[g0]
    speed = m_ref[1]
    partial_sum = jnp.sum(jnp.sum(speed * speed, axis=1, keepdims=True), axis=0, keepdims=True)
    rate_own = jnp.full((1, 1), 0.25 * f_ref[0].astype(F32), F32)
    send[:, nvar, 0, :] = jnp.broadcast_to(rate_own, (nd, LANES))
    send[:, nvar, 1, :] = jnp.broadcast_to(partial_sum, (nd, LANES))

    recv[mh, ms] = send[me, 0 : nvar + 1]
    mrecv[ms] = send[me, nvar + 1 : nvar + 4]

    pl.semaphore_wait(barrier, nd - 1)

    def out_copy(kd, sd):
        d = kd * ns + sd
        return pltpu.make_async_remote_copy(
            src_ref=send.at[d, pl.ds(0, nvar + 1)],
            dst_ref=recv.at[mh, ms],
            send_sem=hs_sem.at[d],
            recv_sem=hr_sem.at[me],
            device_id=(kd, sd),
            device_id_type=MESH_ID,
        )

    def in_copy(kd, sd):
        d = kd * ns + sd
        return pltpu.make_async_remote_copy(
            src_ref=send.at[d, pl.ds(0, nvar + 1)],
            dst_ref=recv.at[kd, sd],
            send_sem=hs_sem.at[d],
            recv_sem=hr_sem.at[d],
            device_id=(kd, sd),
            device_id_type=MESH_ID,
        )

    def mean_copy(s, slot):
        return pltpu.make_async_remote_copy(
            src_ref=send.at[mh * ns + s, pl.ds(nvar + 1, 3)],
            dst_ref=mrecv.at[slot],
            send_sem=ms_sem.at[s],
            recv_sem=mr_sem.at[slot],
            device_id=(mh, s),
            device_id_type=MESH_ID,
        )

    for oh, os in far_first:
        out_copy(flip(mh, oh), flip(ms, os)).start()
        if oh == 1 and os == ns - 1:
            for o in range(ns - 1, 0, -1):
                mean_copy(flip(ms, o), ms).start()

    lane = lax.broadcasted_iota(jnp.int32, (nx, LANES), 1)
    cell = lax.broadcasted_iota(jnp.int32, (nx, LANES), 0)
    second = (lane >> 1) & 1
    is_real = second == 0

    def other(value):
        return jnp.where(is_real, pltpu.roll(value, LANES - 2, 1), pltpu.roll(value, 2, 1))

    def spread(value):
        turned = other(value)
        return jnp.where(is_real, value, turned), jnp.where(is_real, turned, value)

    for o in range(1, ns):
        peer = flip(ms, o)
        in_copy(mh, peer).wait_recv()
        mean_copy(peer, peer).wait_recv()
    packed = []
    for b in range(3):
        for s in range(ns):
            mean[b, cells * s : cells * s + cells, :] = mrecv[s, b]
        packed.append(mean[b])
    m4, wall = spread(packed[0])
    m0, m1 = spread(packed[1])
    m2, m3 = spread(packed[2])
    for a, value in enumerate((m0, m1, m2, m3, m4)):
        mean[a] = value
        mean0[a] = value
    total = recv[mh, 0, nvar, 1:2, :]
    for s in range(1, ns):
        total = total + recv[mh, s, nvar, 1:2, :]
    count = nx * tiles * LANES
    time_step = jnp.broadcast_to(0.9 / (1.0 + jnp.sqrt(total / count)), (nx, LANES))
    wall2 = 2.0 * wall
    z = (lane & 1) * nd + me
    radius = 0.5 + (z.astype(F32) + 0.5) / (2 * nd)
    inv_r = 1.0 / radius

    mp1 = jnp.where(cell < nx - 1, 1.0, 0.0).astype(F32)
    mm1 = jnp.where(cell > 0, 1.0, 0.0).astype(F32)
    mp2 = jnp.where(cell < nx - 2, 1.0, 0.0).astype(F32)
    mm2 = jnp.where(cell > 1, 1.0, 0.0).astype(F32)

    def xp(v, n):
        return pltpu.roll(v, nx - n, 0)

    def xm(v, n):
        return pltpu.roll(v, n, 0)

    def yp(v, n):
        return pltpu.roll(v, LANES - 4 * n, 1)

    def ym(v, n):
        return pltpu.roll(v, 4 * n, 1)

    def pieces(v, fwd, bwd):
        xp1, xm1 = xp(v, 1), xm(v, 1)
        yp1, ym1 = yp(v, 1), ym(v, 1)
        fourth = (
            mp2 * xp(v, 2) + mm2 * xm(v, 2) + 12.0 * v + yp(v, 2) + ym(v, 2)
            - 4.0 * (mp1 * xp1 + mm1 * xm1 + yp1 + ym1)
        )
        return fwd * xp1 - bwd * xm1, yp1 - ym1, fourth

    def mix(us, vs, a):
        flux = jx_ref[a, 0] * us[0]
        for b in range(1, nvar):
            flux = flux + jx_ref[a, b] * us[b]
        for b in range(nvar):
            flux = flux + jy_ref[a, b] * vs[b]
        return 0.5 * flux

    pairs = ((1, 1), (1, 2), (1, 3), (2, 2), (2, 3), (3, 3), (4, 1), (4, 2), (4, 3))

    zero = jnp.zeros((nx, LANES), F32)
    empty = (zero,) * len(pairs)

    def products(acc, hs):
        return tuple(s + hs[p] * hs[q] for s, (p, q) in zip(acc, pairs))

    def advance(k, hs, om, edges, step):
        om = jnp.where(is_real, om, -om)
        got = [pieces(h, *edges) for h in hs]
        us, vs = [g[0] for g in got], [g[1] for g in got]
        news = []
        for a in range(nvar):
            res = om * other(hs[a]) - mix(us, vs, a) - 0.05 * got[a][2] - wall2 * hs[a]
            news.append(first[k, a] + step * res)
        return news

    def edges_of(mc):
        return mp1 * xp(mc, 1), mm1 * xm(mc, 1)

    def gx(v):
        return 0.5 * (mp1 * xp(v, 1) - mm1 * xm(v, 1))

    def gy(v):
        return 0.5 * (yp(v, 1) - ym(v, 1))

    def advance_mean(acc, step):
        s = [0.5 * (v + other(v)) for v in acc]
        force = (
            zero,
            -gx(s[0]) - gy(s[1]),
            -gx(s[1]) - gy(s[3]) - 2.0 * s[4] * inv_r,
            -gx(s[2]) - gy(s[4]) + (s[3] - s[5]) * inv_r,
            -gx(s[6]) - gy(s[7]) - s[8] * inv_r,
        )
        got = [pieces(mean[a], mp1, mm1) for a in range(nvar)]
        us, vs = [g[0] for g in got], [g[1] for g in got]
        for a in range(nvar):
            res = force[a] - mix(us, vs, a) - 0.05 * got[a][2]
            mean[a] = mean0[a] + step * res

    edges = edges_of(mean[1])
    step = SECTION_RATES[0] * time_step

    def landed(k, accs):
        before, after = accs
        for s in range(ns):
            for a in range(nvar):
                first[k, a, cells * s : cells * s + cells, :] = recv[k, s, a]
        om = jnp.broadcast_to(recv[k, 0, nvar, 0:1, :], (nx, LANES))
        omega[k] = om
        hs = [first[k, a] for a in range(nvar)]
        news = advance(k, hs, om, edges, step)
        for a in range(nvar):
            state[k, a] = news[a]
        return products(before, hs), products(after, news)

    def arrive(o, accs):
        k = flip_by(mh, o)
        for os in range(ns):
            in_copy(k, flip(ms, os)).wait_recv()
        return landed(k, accs)

    before, acc = lax.fori_loop(1, nh, arrive, landed(mh, (empty, empty)))
    advance_mean(before, step)

    def section(i, acc):
        step = jnp.where(i == 1, SECTION_RATES[1], SECTION_RATES[2]).astype(F32) * time_step
        edges = edges_of(mean[1])

        def one(k, after):
            news = advance(k, [state[k, a] for a in range(nvar)], omega[k], edges, step)
            for a in range(nvar):
                state[k, a] = news[a]
            return products(after, news)

        after = lax.fori_loop(0, nh, one, empty, unroll=4)
        advance_mean(acc, step)
        return after

    acc = lax.fori_loop(1, 3, section, acc)

    step = SECTION_RATES[3] * time_step
    edges = edges_of(mean[1])
    advance_mean(acc, step)

    def join(even, odd):
        return jnp.where(is_real, even, odd)

    packs = (mean[4], join(mean[0], mean[1]), join(mean[2], mean[3]))

    def back_copy(k, s, slot):
        d = k * ns + s
        return pltpu.make_async_remote_copy(
            src_ref=back.at[k, s],
            dst_ref=home.at[slot],
            send_sem=bs_sem.at[d],
            recv_sem=br_sem.at[slot],
            device_id=(k, s),
            device_id_type=MESH_ID,
        )

    def finish(k):
        news = advance(k, [state[k, a] for a in range(nvar)], omega[k], edges, step)
        for s in range(ns):
            for a in range(nvar):
                back[k, s, a] = news[a][cells * s : cells * s + cells, :]
            for b in range(3):
                back[k, s, nvar + b] = packs[b][cells * s : cells * s + cells, :]

    def depart(o, _):
        k = flip_by(mh, nh - 1 - o)
        finish(k)
        for os in range(ns - 1, -1, -1):
            back_copy(k, flip(ms, os), me).start()
        return 0

    lax.fori_loop(0, nh - 1, depart, 0)
    finish(mh)
    for os in range(ns - 1, 0, -1):
        back_copy(mh, flip(ms, os), me).start()
    own = pltpu.make_async_copy(back.at[mh, ms], home.at[me], own_sem)
    own.start()

    def land_back(o, _):
        d = lax.rem(me + o, nd)
        back_copy(d // ns, lax.rem(d, ns), d).wait_recv()
        return 0

    lax.fori_loop(1, nd, land_back, 0)

    own.wait()

    def sent(o, _):
        d = lax.rem(me + o, nd)
        out_copy(d // ns, lax.rem(d, ns)).wait_send()
        back_copy(d // ns, lax.rem(d, ns), me).wait_send()
        return 0

    lax.fori_loop(1, nd, sent, 0)
    for o in range(1, ns):
        mean_copy(flip(ms, o), ms).wait_send()


def gather_kernel(dims, home, mo_ref, ho_ref, rows):
    nh, ns, nvar, cells, tiles = dims
    nd = nh * ns
    lane_all = lax.broadcasted_iota(jnp.int32, (nd, LANES), 1)
    low_bit = lane_all & 1
    high_bit = (lane_all >> 2) & 1

    for grp in range(4):
        cols = []
        for g1 in range(2):
            cols.append(swap_bit([home[:, 2 * grp + g1, g0, :] for g0 in range(2)], 1, low_bit))
        part = [swap_bit((cols[0][j], cols[1][j]), 4, high_bit) for j in range(2)]
        mat = jnp.concatenate([part[j][i] for i in range(2) for j in range(2)], axis=0)
        turned = mat.T
        for t in range(tiles):
            rows[ROWS * grp : ROWS * grp + ROWS, LANES * t : LANES * t + LANES] = turned[
                ROWS * t : ROWS * t + ROWS
            ]

    def take(at):
        return rows[pl.ds(cells * at, cells), :]

    for a in range(nvar):
        for c in range(2):
            ho_ref[0, c, a] = take(2 * a + c)
    mo_ref[nvar - 1] = take(2 * nvar)
    for a in range(nvar - 1):
        mo_ref[a] = take(2 * nvar + 2 + a)


def radial_shards(nh, ns, harmonics, mean_flow, freq_index, wall_mask, jacobian_x, jacobian_y):
    nvar, cells, planes = mean_flow.shape
    nd, nx = nh * ns, ns * cells
    vmem = pl.BlockSpec(memory_space=pltpu.VMEM)
    smem = pl.BlockSpec(memory_space=pltpu.SMEM)
    anywhere = pl.BlockSpec(memory_space=pl.ANY)
    dims = (nh, ns, nvar, cells, planes // LANES)
    field = (nx, LANES)
    piece = (cells, LANES)
    home = pl.pallas_call(
        functools.partial(radial_kernel, dims),
        out_shape=jax.ShapeDtypeStruct((nd, nvar + 3, *piece), F32),
        in_specs=[anywhere, anywhere, smem, anywhere, smem, smem],
        out_specs=anywhere,
        scratch_shapes=[
            pltpu.VMEM(harmonics.shape, F32),
            pltpu.VMEM(mean_flow.shape, F32),
            pltpu.VMEM(wall_mask.shape, jnp.int32),
            pltpu.SemaphoreType.DMA((3,)),
            pltpu.VMEM((4 * ROWS, planes), F32),
            pltpu.VMEM((nd, nvar + 4, *piece), F32),
            pltpu.VMEM((nh, ns, nvar + 1, *piece), F32),
            pltpu.VMEM((ns, 3, *piece), F32),
            pltpu.VMEM((nh, nvar, *field), F32),
            pltpu.VMEM((nh, nvar, *field), F32),
            pltpu.VMEM((nh, *field), F32),
            pltpu.VMEM((nvar, *field), F32),
            pltpu.VMEM((nvar, *field), F32),
            pltpu.VMEM((nh, ns, nvar + 3, *piece), F32),
            pltpu.SemaphoreType.DMA,
            pltpu.SemaphoreType.DMA((nd,)),
            pltpu.SemaphoreType.DMA((nd,)),
            pltpu.SemaphoreType.DMA((ns,)),
            pltpu.SemaphoreType.DMA((ns,)),
            pltpu.SemaphoreType.DMA((nd,)),
            pltpu.SemaphoreType.DMA((nd,)),
        ],
        compiler_params=pltpu.CompilerParams(collective_id=0, has_side_effects=True),
    )(harmonics, mean_flow, freq_index, wall_mask, jacobian_x, jacobian_y)
    return pl.pallas_call(
        functools.partial(gather_kernel, dims),
        out_shape=(
            jax.ShapeDtypeStruct(mean_flow.shape, F32),
            jax.ShapeDtypeStruct(harmonics.shape, F32),
        ),
        in_specs=[vmem],
        out_specs=(vmem, vmem),
        scratch_shapes=[pltpu.VMEM((4 * ROWS, planes), F32)],
    )(home)


def fits_radial(nh, ns, harmonics, mean_flow):
    owned, parts, nvar, cells, planes = harmonics.shape
    return (
        NZ == 2 * nh * ns
        and LANES == 2 * NZ
        and (owned, parts, nvar, cells) == (1, 2, 5, 2)
        and ns * cells == ROWS
        and planes == 16 * LANES
    )


def either(nh, ns, harmonics, mean_flow, *rest):
    if fits_radial(nh, ns, harmonics, mean_flow):
        return radial_shards(nh, ns, harmonics, mean_flow, *rest)
    return shards(harmonics, mean_flow, *rest)


def solution(mesh):
    placed = (
        P("harm", None, None, "slab", None),
        P(None, "slab", None),
        P("harm"),
        P("slab", None),
        P(),
        P(),
    )
    return jax.shard_map(
        functools.partial(either, mesh.shape["harm"], mesh.shape["slab"]),
        mesh=mesh,
        in_specs=placed,
        out_specs=(P(None, "slab", None), P("harm", None, None, "slab", None)),
        check_vma=False,
    )
```

```python
import functools

import jax
import jax.numpy as jnp
from jax import lax
from jax.experimental import pallas as pl
from jax.experimental.pallas import tpu as pltpu
from jax.sharding import PartitionSpec as P

NZ = 64


EPS_FOURTH = 0.05
COURANT = 0.9
OMEGA_BASE = 0.25
WALL_RATE = 2.0
HUB_RADIUS = 0.5
SECTION_RATES = (0.25, 1.0 / 3.0, 0.5, 1.0)
STRESS_PAIRS = ((1, 1), (1, 2), (1, 3), (2, 2), (2, 3), (3, 3), (4, 1), (4, 2), (4, 3))


def with_halo(cells, sides, width):
    for axis, dim in sides:
        count = lax.axis_size(axis)
        ends = count - 1
        head = lax.slice_in_dim(cells, 0, width, axis=dim)
        tail = lax.slice_in_dim(cells, cells.shape[dim] - width, cells.shape[dim], axis=dim)
        cells = jnp.concatenate(
            [
                lax.ppermute(tail, axis, [(i, (i + 1) % count) for i in range(ends)]),
                cells,
                lax.ppermute(head, axis, [((i + 1) % count, i) for i in range(ends)]),
            ],
            axis=dim,
        )
    return cells


def apply_matrix(matrix, values):
    return jnp.einsum("ab,...bxp->...axp", matrix, values, precision=lax.Precision.HIGHEST)


def diff_across(values):
    return (jnp.roll(values, -NZ, axis=-1) - jnp.roll(values, NZ, axis=-1)) * 0.5


def fourth_across(values):
    return (
        jnp.roll(values, -2 * NZ, axis=-1)
        - 4.0 * jnp.roll(values, -NZ, axis=-1)
        + 6.0 * values
        - 4.0 * jnp.roll(values, NZ, axis=-1)
        + jnp.roll(values, 2 * NZ, axis=-1)
    )


def diff_along(padded):
    return (padded[..., 3:-1, :] - padded[..., 1:-3, :]) * 0.5


def fourth_along(padded):
    return (
        padded[..., 4:, :]
        - 4.0 * padded[..., 3:-1, :]
        + 6.0 * padded[..., 2:-2, :]
        - 4.0 * padded[..., 1:-3, :]
        + padded[..., :-4, :]
    )


def harmonic_residual(harm_pad, momentum_pad, omegas, wall_cells, jac_x, jac_y):
    center = harm_pad[..., 2:-2, :]
    flux_x = apply_matrix(jac_x, harm_pad * momentum_pad)
    flux_y = apply_matrix(jac_y, center)
    rotation = jnp.stack([center[..., 1, :, :, :], -center[..., 0, :, :, :]], axis=-4) * omegas
    return (
        rotation
        - diff_along(flux_x)
        - diff_across(flux_y)
        - EPS_FOURTH * (fourth_along(harm_pad) + fourth_across(center))
        - WALL_RATE * wall_cells * center
    )


def stresses(values):
    fields = []
    for first, second in STRESS_PAIRS:
        product = values[..., first, :, :] * values[..., second, :, :]
        fields.append(0.5 * jnp.sum(product, axis=tuple(range(product.ndim - 2))))
    return jnp.stack(fields, axis=0)


def forcing(stress_pad, radius):
    center = stress_pad[:, 1:-1, :]
    grad_x = (stress_pad[:, 2:, :] - stress_pad[:, :-2, :]) * 0.5
    grad_y = diff_across(center)
    first = -grad_x[0] - grad_y[1]
    second = -grad_x[1] - grad_y[3] - 2.0 * center[4] / radius
    third = -grad_x[2] - grad_y[4] + (center[3] - center[5]) / radius
    fourth = -grad_x[6] - grad_y[7] - center[8] / radius
    return jnp.stack([first, second, third, fourth], axis=0)


def mean_residual(mean_pad, forcing_terms, jac_x, jac_y):
    center = mean_pad[:, 2:-2, :]
    residual = (
        -diff_along(apply_matrix(jac_x, mean_pad))
        - diff_across(apply_matrix(jac_y, center))
        - EPS_FOURTH * (fourth_along(mean_pad) + fourth_across(center))
    )
    zeros_row = jnp.zeros_like(forcing_terms[:1])
    return residual + jnp.concatenate([zeros_row, forcing_terms], axis=0)


def shards(harmonics, mean_flow, freq_index, wall_mask, jacobian_x, jacobian_y):
    owned = harmonics.shape[0]
    slab_cells = mean_flow.shape[1]
    plane_count = mean_flow.shape[2]
    radius = HUB_RADIUS + ((jnp.arange(plane_count) % NZ).astype(jnp.float32) + 0.5) / NZ
    wall_cells = wall_mask.astype(jnp.float32)
    omegas = (OMEGA_BASE * freq_index.astype(jnp.float32)).reshape(owned, 1, 1, 1, 1)
    speed_total = lax.psum(jnp.sum(mean_flow[1] * mean_flow[1]), "slab")
    cell_count = slab_cells * lax.axis_size("slab") * plane_count
    time_step = COURANT / (1.0 + jnp.sqrt(speed_total / cell_count))
    harm_now, mean_now = (harmonics, mean_flow)
    for section_rate in SECTION_RATES:
        stacked = jnp.concatenate(
            [harm_now.reshape(owned * 2, 5, slab_cells, plane_count), mean_now[None]], axis=0
        )
        padded = with_halo(stacked, (("slab", 2),), 2)
        harm_pad = padded[: 2 * owned].reshape(owned, 2, 5, slab_cells + 4, plane_count)
        mean_pad = padded[2 * owned]
        harm_res = harmonic_residual(
            harm_pad, mean_pad[1], omegas, wall_cells, jacobian_x, jacobian_y
        )
        partial_terms = forcing(stresses(harm_pad[..., 1:-1, :]), radius)
        forcing_terms = lax.psum(partial_terms, "harm")
        mean_res = mean_residual(mean_pad, forcing_terms, jacobian_x, jacobian_y)
        harm_now = harmonics + section_rate * time_step * harm_res
        mean_now = mean_flow + section_rate * time_step * mean_res
    return (mean_now, harm_now)


MESH_ID = pl.DeviceIdType.MESH
LANES = 128
ROWS = 8
F32 = jnp.float32


def swap_bit(pair, stride, bit):
    low, high = pair
    return (
        jnp.where(bit == 0, low, pltpu.roll(high, stride, 1)),
        jnp.where(bit == 0, pltpu.roll(low, LANES - stride, 1), high),
    )


def radial_kernel(
    dims, h_any, m_any, f_ref, w_any, jx_ref, jy_ref, home,
    h_ref, m_ref, w_ref, in_sem, rows, send, recv, mrecv, state, first, omega, mean, mean0, back, own_sem,
    hs_sem, hr_sem, ms_sem, mr_sem, bs_sem, br_sem,
):
    nh, ns, nvar, cells, tiles = dims
    nd = nh * ns
    mh, ms = lax.axis_index("harm"), lax.axis_index("slab")
    me = mh * ns + ms
    nx = ns * cells

    barrier = pltpu.get_barrier_semaphore()

    def flip(index, bits):
        out = index
        weight = 1
        while weight <= bits:
            if bits & weight:
                out = out + weight * (1 - 2 * lax.rem(index // weight, 2))
            weight *= 2
        return out

    def flip_by(index, bits):
        out = index
        weight = 1
        while weight < nh:
            out = out + lax.rem(bits // weight, 2) * weight * (1 - 2 * lax.rem(index // weight, 2))
            weight *= 2
        return out

    def reach(offset):
        oh, os = offset
        return min(oh >> 1, 2) + (oh & 1) + (os >> 1) + 0.3 * (os & 1)

    far_first = sorted(
        [(oh, os) for oh in range(nh) for os in range(ns) if oh or os], key=reach, reverse=True
    )
    for oh, os in far_first:
        pl.semaphore_signal(
            barrier, inc=1, device_id=(flip(mh, oh), flip(ms, os)), device_id_type=MESH_ID
        )
    loads = [
        pltpu.make_async_copy(src, dst, in_sem.at[i])
        for i, (src, dst) in enumerate(((h_any, h_ref), (m_any, m_ref), (w_any, w_ref)))
    ]
    for load in loads:
        load.start()
    for load in loads:
        load.wait()

    lane_all = lax.broadcasted_iota(jnp.int32, (nd, LANES), 1)
    low_bit = lane_all & 1
    high_bit = (lane_all >> 2) & 1

    def place(at, value):
        rows[pl.ds(cells * at, cells), :] = value

    for a in range(nvar):
        for c in range(2):
            place(2 * a + c, h_ref[0, c, a])
    place(2 * nvar, m_ref[nvar - 1])
    place(2 * nvar + 1, w_ref[...].astype(F32))
    for a in range(nvar - 1):
        place(2 * nvar + 2 + a, m_ref[a])

    def block_of(g):
        return g if g < nvar else g + 1

    for grp in range(4):
        mat = jnp.concatenate(
            [rows[ROWS * grp : ROWS * grp + ROWS, LANES * t : LANES * t + LANES] for t in range(tiles)],
            axis=0,
        )
        turned = mat.T
        part = [[turned[nd * (2 * i + j) : nd * (2 * i + j) + nd] for j in range(2)] for i in range(2)]
        cols = [swap_bit((part[0][j], part[1][j]), 4, high_bit) for j in range(2)]
        for g1 in range(2):
            outs = swap_bit((cols[0][g1], cols[1][g1]), 1, low_bit)
            for g0 in range(2):
                send[:, block_of(2 * grp + g1), g0, :] = outs[g0]
    speed = m_ref[1]
    partial_sum = jnp.sum(jnp.sum(speed * speed, axis=1, keepdims=True), axis=0, keepdims=True)
    rate_own = jnp.full((1, 1), 0.25 * f_ref[0].astype(F32), F32)
    send[:, nvar, 0, :] = jnp.broadcast_to(rate_own, (nd, LANES))
    send[:, nvar, 1, :] = jnp.broadcast_to(partial_sum, (nd, LANES))

    recv[mh, ms] = send[me, 0 : nvar + 1]
    mrecv[ms] = send[me, nvar + 1 : nvar + 4]

    pl.semaphore_wait(barrier, nd - 1)

    def out_copy(kd, sd):
        d = kd * ns + sd
        return pltpu.make_async_remote_copy(
            src_ref=send.at[d, pl.ds(0, nvar + 1)],
            dst_ref=recv.at[mh, ms],
            send_sem=hs_sem.at[d],
            recv_sem=hr_sem.at[me],
            device_id=(kd, sd),
            device_id_type=MESH_ID,
        )

    def in_copy(kd, sd):
        d = kd * ns + sd
        return pltpu.make_async_remote_copy(
            src_ref=send.at[d, pl.ds(0, nvar + 1)],
            dst_ref=recv.at[kd, sd],
            send_sem=hs_sem.at[d],
            recv_sem=hr_sem.at[d],
            device_id=(kd, sd),
            device_id_type=MESH_ID,
        )

    def mean_copy(s, slot):
        return pltpu.make_async_remote_copy(
            src_ref=send.at[mh * ns + s, pl.ds(nvar + 1, 3)],
            dst_ref=mrecv.at[slot],
            send_sem=ms_sem.at[s],
            recv_sem=mr_sem.at[slot],
            device_id=(mh, s),
            device_id_type=MESH_ID,
        )

    for oh, os in far_first:
        out_copy(flip(mh, oh), flip(ms, os)).start()
        if oh == 1 and os == ns - 1:
            for o in range(ns - 1, 0, -1):
                mean_copy(flip(ms, o), ms).start()

    lane = lax.broadcasted_iota(jnp.int32, (nx, LANES), 1)
    cell = lax.broadcasted_iota(jnp.int32, (nx, LANES), 0)
    second = (lane >> 1) & 1
    is_real = second == 0

    def other(value):
        return jnp.where(is_real, pltpu.roll(value, LANES - 2, 1), pltpu.roll(value, 2, 1))

    def spread(value):
        turned = other(value)
        return jnp.where(is_real, value, turned), jnp.where(is_real, turned, value)

    for o in range(1, ns):
        peer = flip(ms, o)
        in_copy(mh, peer).wait_recv()
        mean_copy(peer, peer).wait_recv()
    packed = []
    for b in range(3):
        for s in range(ns):
            mean[b, cells * s : cells * s + cells, :] = mrecv[s, b]
        packed.append(mean[b])
    m4, wall = spread(packed[0])
    m0, m1 = spread(packed[1])
    m2, m3 = spread(packed[2])
    for a, value in enumerate((m0, m1, m2, m3, m4)):
        mean[a] = value
        mean0[a] = value
    total = recv[mh, 0, nvar, 1:2, :]
    for s in range(1, ns):
        total = total + recv[mh, s, nvar, 1:2, :]
    count = nx * tiles * LANES
    time_step = jnp.broadcast_to(0.9 / (1.0 + jnp.sqrt(total / count)), (nx, LANES))
    wall2 = 2.0 * wall
    z = (lane & 1) * nd + me
    radius = 0.5 + (z.astype(F32) + 0.5) / (2 * nd)
    inv_r = 1.0 / radius

    mp1 = jnp.where(cell < nx - 1, 1.0, 0.0).astype(F32)
    mm1 = jnp.where(cell > 0, 1.0, 0.0).astype(F32)
    mp2 = jnp.where(cell < nx - 2, 1.0, 0.0).astype(F32)
    mm2 = jnp.where(cell > 1, 1.0, 0.0).astype(F32)

    def xp(v, n):
        return pltpu.roll(v, nx - n, 0)

    def xm(v, n):
        return pltpu.roll(v, n, 0)

    def yp(v, n):
        return pltpu.roll(v, LANES - 4 * n, 1)

    def ym(v, n):
        return pltpu.roll(v, 4 * n, 1)

    def pieces(v, fwd, bwd):
        xp1, xm1 = xp(v, 1), xm(v, 1)
        yp1, ym1 = yp(v, 1), ym(v, 1)
        fourth = (
            mp2 * xp(v, 2) + mm2 * xm(v, 2) + 12.0 * v + yp(v, 2) + ym(v, 2)
            - 4.0 * (mp1 * xp1 + mm1 * xm1 + yp1 + ym1)
        )
        return fwd * xp1 - bwd * xm1, yp1 - ym1, fourth

    def mix(us, vs, a):
        flux = jx_ref[a, 0] * us[0]
        for b in range(1, nvar):
            flux = flux + jx_ref[a, b] * us[b]
        for b in range(nvar):
            flux = flux + jy_ref[a, b] * vs[b]
        return 0.5 * flux

    pairs = ((1, 1), (1, 2), (1, 3), (2, 2), (2, 3), (3, 3), (4, 1), (4, 2), (4, 3))

    zero = jnp.zeros((nx, LANES), F32)
    empty = (zero,) * len(pairs)

    def products(acc, hs):
        return tuple(s + hs[p] * hs[q] for s, (p, q) in zip(acc, pairs))

    def advance(k, hs, om, edges, step):
        om = jnp.where(is_real, om, -om)
        got = [pieces(h, *edges) for h in hs]
        us, vs = [g[0] for g in got], [g[1] for g in got]
        news = []
        for a in range(nvar):
            res = om * other(hs[a]) - mix(us, vs, a) - 0.05 * got[a][2] - wall2 * hs[a]
            news.append(first[k, a] + step * res)
        return news

    def edges_of(mc):
        return mp1 * xp(mc, 1), mm1 * xm(mc, 1)

    def gx(v):
        return 0.5 * (mp1 * xp(v, 1) - mm1 * xm(v, 1))

    def gy(v):
        return 0.5 * (yp(v, 1) - ym(v, 1))

    def advance_mean(acc, step):
        s = [0.5 * (v + other(v)) for v in acc]
        force = (
            zero,
            -gx(s[0]) - gy(s[1]),
            -gx(s[1]) - gy(s[3]) - 2.0 * s[4] * inv_r,
            -gx(s[2]) - gy(s[4]) + (s[3] - s[5]) * inv_r,
            -gx(s[6]) - gy(s[7]) - s[8] * inv_r,
        )
        got = [pieces(mean[a], mp1, mm1) for a in range(nvar)]
        us, vs = [g[0] for g in got], [g[1] for g in got]
        for a in range(nvar):
            res = force[a] - mix(us, vs, a) - 0.05 * got[a][2]
            mean[a] = mean0[a] + step * res

    edges = edges_of(mean[1])
    step = SECTION_RATES[0] * time_step

    def landed(k, accs):
        before, after = accs
        for s in range(ns):
            for a in range(nvar):
                first[k, a, cells * s : cells * s + cells, :] = recv[k, s, a]
        om = jnp.broadcast_to(recv[k, 0, nvar, 0:1, :], (nx, LANES))
        omega[k] = om
        hs = [first[k, a] for a in range(nvar)]
        news = advance(k, hs, om, edges, step)
        for a in range(nvar):
            state[k, a] = news[a]
        return products(before, hs), products(after, news)

    def arrive(o, accs):
        k = flip_by(mh, o)
        for os in range(ns):
            in_copy(k, flip(ms, os)).wait_recv()
        return landed(k, accs)

    before, acc = lax.fori_loop(1, nh, arrive, landed(mh, (empty, empty)), unroll=nh - 1)
    advance_mean(before, step)

    def section(i, acc):
        step = jnp.where(i == 1, SECTION_RATES[1], SECTION_RATES[2]).astype(F32) * time_step
        edges = edges_of(mean[1])

        def one(k, after):
            news = advance(k, [state[k, a] for a in range(nvar)], omega[k], edges, step)
            for a in range(nvar):
                state[k, a] = news[a]
            return products(after, news)

        after = lax.fori_loop(0, nh, one, empty, unroll=nh)
        advance_mean(acc, step)
        return after

    acc = lax.fori_loop(1, 3, section, acc)

    step = SECTION_RATES[3] * time_step
    edges = edges_of(mean[1])
    advance_mean(acc, step)

    def join(even, odd):
        return jnp.where(is_real, even, odd)

    packs = (mean[4], join(mean[0], mean[1]), join(mean[2], mean[3]))

    def back_copy(k, s, slot):
        d = k * ns + s
        return pltpu.make_async_remote_copy(
            src_ref=back.at[k, s],
            dst_ref=home.at[slot],
            send_sem=bs_sem.at[d],
            recv_sem=br_sem.at[slot],
            device_id=(k, s),
            device_id_type=MESH_ID,
        )

    def finish(k):
        news = advance(k, [state[k, a] for a in range(nvar)], omega[k], edges, step)
        for s in range(ns):
            for a in range(nvar):
                back[k, s, a] = news[a][cells * s : cells * s + cells, :]
            for b in range(3):
                back[k, s, nvar + b] = packs[b][cells * s : cells * s + cells, :]

    def depart(o, _):
        k = flip_by(mh, nh - 1 - o)
        finish(k)
        for os in range(ns - 1, -1, -1):
            back_copy(k, flip(ms, os), me).start()
        return 0

    lax.fori_loop(0, nh - 1, depart, 0, unroll=nh - 1)
    finish(mh)
    for os in range(ns - 1, 0, -1):
        back_copy(mh, flip(ms, os), me).start()
    own = pltpu.make_async_copy(back.at[mh, ms], home.at[me], own_sem)
    own.start()

    def land_back(o, _):
        d = lax.rem(me + o, nd)
        back_copy(d // ns, lax.rem(d, ns), d).wait_recv()
        return 0

    lax.fori_loop(1, nd, land_back, 0)

    own.wait()

    def sent(o, _):
        d = lax.rem(me + o, nd)
        out_copy(d // ns, lax.rem(d, ns)).wait_send()
        back_copy(d // ns, lax.rem(d, ns), me).wait_send()
        return 0

    lax.fori_loop(1, nd, sent, 0)
    for o in range(1, ns):
        mean_copy(flip(ms, o), ms).wait_send()


def gather_kernel(dims, home_any, mo_any, ho_any, home, mo_ref, ho_ref, rows, in_sem, out_sem):
    nh, ns, nvar, cells, tiles = dims
    nd = nh * ns
    lane_all = lax.broadcasted_iota(jnp.int32, (nd, LANES), 1)
    low_bit = lane_all & 1
    high_bit = (lane_all >> 2) & 1

    loads = [
        pltpu.make_async_copy(
            home_any.at[:, pl.ds(2 * g, 2)], home.at[:, pl.ds(2 * g, 2)], in_sem.at[g]
        )
        for g in range(4)
    ]
    stores = []
    for load in loads:
        load.start()

    def take(at):
        return rows[pl.ds(cells * at, cells), :]

    for grp in range(4):
        loads[grp].wait()
        cols = []
        for g1 in range(2):
            cols.append(swap_bit([home[:, 2 * grp + g1, g0, :] for g0 in range(2)], 1, low_bit))
        part = [swap_bit((cols[0][j], cols[1][j]), 4, high_bit) for j in range(2)]
        mat = jnp.concatenate([part[j][i] for i in range(2) for j in range(2)], axis=0)
        turned = mat.T
        for t in range(tiles):
            rows[ROWS * grp : ROWS * grp + ROWS, LANES * t : LANES * t + LANES] = turned[
                ROWS * t : ROWS * t + ROWS
            ]
        for pair in (2 * grp, 2 * grp + 1):
            for c in range(2):
                if pair < nvar:
                    ho_ref[0, c, pair] = take(2 * pair + c)
                elif pair == nvar:
                    mo_ref[nvar - 1] = take(2 * pair)
                    break
                else:
                    mo_ref[2 * (pair - nvar - 1) + c] = take(2 * pair + c)
        if 2 * grp < nvar:
            count = min(2, nvar - 2 * grp)
            part_of = (0, slice(None), pl.ds(2 * grp, count))
            stores.append(
                pltpu.make_async_copy(ho_ref.at[part_of], ho_any.at[part_of], out_sem.at[grp])
            )
            stores[-1].start()
    stores.append(pltpu.make_async_copy(mo_ref, mo_any, out_sem.at[3]))
    stores[-1].start()
    for store in stores:
        store.wait()


def radial_shards(nh, ns, harmonics, mean_flow, freq_index, wall_mask, jacobian_x, jacobian_y):
    nvar, cells, planes = mean_flow.shape
    nd, nx = nh * ns, ns * cells
    smem = pl.BlockSpec(memory_space=pltpu.SMEM)
    anywhere = pl.BlockSpec(memory_space=pl.ANY)
    dims = (nh, ns, nvar, cells, planes // LANES)
    field = (nx, LANES)
    piece = (cells, LANES)
    home = pl.pallas_call(
        functools.partial(radial_kernel, dims),
        out_shape=jax.ShapeDtypeStruct((nd, nvar + 3, *piece), F32),
        in_specs=[anywhere, anywhere, smem, anywhere, smem, smem],
        out_specs=anywhere,
        scratch_shapes=[
            pltpu.VMEM(harmonics.shape, F32),
            pltpu.VMEM(mean_flow.shape, F32),
            pltpu.VMEM(wall_mask.shape, jnp.int32),
            pltpu.SemaphoreType.DMA((3,)),
            pltpu.VMEM((4 * ROWS, planes), F32),
            pltpu.VMEM((nd, nvar + 4, *piece), F32),
            pltpu.VMEM((nh, ns, nvar + 1, *piece), F32),
            pltpu.VMEM((ns, 3, *piece), F32),
            pltpu.VMEM((nh, nvar, *field), F32),
            pltpu.VMEM((nh, nvar, *field), F32),
            pltpu.VMEM((nh, *field), F32),
            pltpu.VMEM((nvar, *field), F32),
            pltpu.VMEM((nvar, *field), F32),
            pltpu.VMEM((nh, ns, nvar + 3, *piece), F32),
            pltpu.SemaphoreType.DMA,
            pltpu.SemaphoreType.DMA((nd,)),
            pltpu.SemaphoreType.DMA((nd,)),
            pltpu.SemaphoreType.DMA((ns,)),
            pltpu.SemaphoreType.DMA((ns,)),
            pltpu.SemaphoreType.DMA((nd,)),
            pltpu.SemaphoreType.DMA((nd,)),
        ],
        compiler_params=pltpu.CompilerParams(collective_id=0, has_side_effects=True),
    )(harmonics, mean_flow, freq_index, wall_mask, jacobian_x, jacobian_y)
    return pl.pallas_call(
        functools.partial(gather_kernel, dims),
        out_shape=(
            jax.ShapeDtypeStruct(mean_flow.shape, F32),
            jax.ShapeDtypeStruct(harmonics.shape, F32),
        ),
        in_specs=[anywhere],
        out_specs=(anywhere, anywhere),
        scratch_shapes=[
            pltpu.VMEM((nd, nvar + 3, *piece), F32),
            pltpu.VMEM(mean_flow.shape, F32),
            pltpu.VMEM(harmonics.shape, F32),
            pltpu.VMEM((4 * ROWS, planes), F32),
            pltpu.SemaphoreType.DMA((4,)),
            pltpu.SemaphoreType.DMA((4,)),
        ],
    )(home)


def fits_radial(nh, ns, harmonics, mean_flow):
    owned, parts, nvar, cells, planes = harmonics.shape
    return (
        NZ == 2 * nh * ns
        and LANES == 2 * NZ
        and (owned, parts, nvar, cells) == (1, 2, 5, 2)
        and ns * cells == ROWS
        and planes == 16 * LANES
    )


def either(nh, ns, harmonics, mean_flow, *rest):
    if fits_radial(nh, ns, harmonics, mean_flow):
        return radial_shards(nh, ns, harmonics, mean_flow, *rest)
    return shards(harmonics, mean_flow, *rest)


def solution(mesh):
    placed = (
        P("harm", None, None, "slab", None),
        P(None, "slab", None),
        P("harm"),
        P("slab", None),
        P(),
        P(),
    )
    return jax.shard_map(
        functools.partial(either, mesh.shape["harm"], mesh.shape["slab"]),
        mesh=mesh,
        in_specs=placed,
        out_specs=(P(None, "slab", None), P("harm", None, None, "slab", None)),
        check_vma=False,
    )
```

```python
import functools

import jax
import jax.numpy as jnp
from jax import lax
from jax.experimental import pallas as pl
from jax.experimental.pallas import tpu as pltpu
from jax.sharding import PartitionSpec as P

NZ = 64


EPS_FOURTH = 0.05
COURANT = 0.9
OMEGA_BASE = 0.25
WALL_RATE = 2.0
HUB_RADIUS = 0.5
SECTION_RATES = (0.25, 1.0 / 3.0, 0.5, 1.0)
STRESS_PAIRS = ((1, 1), (1, 2), (1, 3), (2, 2), (2, 3), (3, 3), (4, 1), (4, 2), (4, 3))


def with_halo(cells, sides, width):
    for axis, dim in sides:
        count = lax.axis_size(axis)
        ends = count - 1
        head = lax.slice_in_dim(cells, 0, width, axis=dim)
        tail = lax.slice_in_dim(cells, cells.shape[dim] - width, cells.shape[dim], axis=dim)
        cells = jnp.concatenate(
            [
                lax.ppermute(tail, axis, [(i, (i + 1) % count) for i in range(ends)]),
                cells,
                lax.ppermute(head, axis, [((i + 1) % count, i) for i in range(ends)]),
            ],
            axis=dim,
        )
    return cells


def apply_matrix(matrix, values):
    return jnp.einsum("ab,...bxp->...axp", matrix, values, precision=lax.Precision.HIGHEST)


def diff_across(values):
    return (jnp.roll(values, -NZ, axis=-1) - jnp.roll(values, NZ, axis=-1)) * 0.5


def fourth_across(values):
    return (
        jnp.roll(values, -2 * NZ, axis=-1)
        - 4.0 * jnp.roll(values, -NZ, axis=-1)
        + 6.0 * values
        - 4.0 * jnp.roll(values, NZ, axis=-1)
        + jnp.roll(values, 2 * NZ, axis=-1)
    )


def diff_along(padded):
    return (padded[..., 3:-1, :] - padded[..., 1:-3, :]) * 0.5


def fourth_along(padded):
    return (
        padded[..., 4:, :]
        - 4.0 * padded[..., 3:-1, :]
        + 6.0 * padded[..., 2:-2, :]
        - 4.0 * padded[..., 1:-3, :]
        + padded[..., :-4, :]
    )


def harmonic_residual(harm_pad, momentum_pad, omegas, wall_cells, jac_x, jac_y):
    center = harm_pad[..., 2:-2, :]
    flux_x = apply_matrix(jac_x, harm_pad * momentum_pad)
    flux_y = apply_matrix(jac_y, center)
    rotation = jnp.stack([center[..., 1, :, :, :], -center[..., 0, :, :, :]], axis=-4) * omegas
    return (
        rotation
        - diff_along(flux_x)
        - diff_across(flux_y)
        - EPS_FOURTH * (fourth_along(harm_pad) + fourth_across(center))
        - WALL_RATE * wall_cells * center
    )


def stresses(values):
    fields = []
    for first, second in STRESS_PAIRS:
        product = values[..., first, :, :] * values[..., second, :, :]
        fields.append(0.5 * jnp.sum(product, axis=tuple(range(product.ndim - 2))))
    return jnp.stack(fields, axis=0)


def forcing(stress_pad, radius):
    center = stress_pad[:, 1:-1, :]
    grad_x = (stress_pad[:, 2:, :] - stress_pad[:, :-2, :]) * 0.5
    grad_y = diff_across(center)
    first = -grad_x[0] - grad_y[1]
    second = -grad_x[1] - grad_y[3] - 2.0 * center[4] / radius
    third = -grad_x[2] - grad_y[4] + (center[3] - center[5]) / radius
    fourth = -grad_x[6] - grad_y[7] - center[8] / radius
    return jnp.stack([first, second, third, fourth], axis=0)


def mean_residual(mean_pad, forcing_terms, jac_x, jac_y):
    center = mean_pad[:, 2:-2, :]
    residual = (
        -diff_along(apply_matrix(jac_x, mean_pad))
        - diff_across(apply_matrix(jac_y, center))
        - EPS_FOURTH * (fourth_along(mean_pad) + fourth_across(center))
    )
    zeros_row = jnp.zeros_like(forcing_terms[:1])
    return residual + jnp.concatenate([zeros_row, forcing_terms], axis=0)


def shards(harmonics, mean_flow, freq_index, wall_mask, jacobian_x, jacobian_y):
    owned = harmonics.shape[0]
    slab_cells = mean_flow.shape[1]
    plane_count = mean_flow.shape[2]
    radius = HUB_RADIUS + ((jnp.arange(plane_count) % NZ).astype(jnp.float32) + 0.5) / NZ
    wall_cells = wall_mask.astype(jnp.float32)
    omegas = (OMEGA_BASE * freq_index.astype(jnp.float32)).reshape(owned, 1, 1, 1, 1)
    speed_total = lax.psum(jnp.sum(mean_flow[1] * mean_flow[1]), "slab")
    cell_count = slab_cells * lax.axis_size("slab") * plane_count
    time_step = COURANT / (1.0 + jnp.sqrt(speed_total / cell_count))
    harm_now, mean_now = (harmonics, mean_flow)
    for section_rate in SECTION_RATES:
        stacked = jnp.concatenate(
            [harm_now.reshape(owned * 2, 5, slab_cells, plane_count), mean_now[None]], axis=0
        )
        padded = with_halo(stacked, (("slab", 2),), 2)
        harm_pad = padded[: 2 * owned].reshape(owned, 2, 5, slab_cells + 4, plane_count)
        mean_pad = padded[2 * owned]
        harm_res = harmonic_residual(
            harm_pad, mean_pad[1], omegas, wall_cells, jacobian_x, jacobian_y
        )
        partial_terms = forcing(stresses(harm_pad[..., 1:-1, :]), radius)
        forcing_terms = lax.psum(partial_terms, "harm")
        mean_res = mean_residual(mean_pad, forcing_terms, jacobian_x, jacobian_y)
        harm_now = harmonics + section_rate * time_step * harm_res
        mean_now = mean_flow + section_rate * time_step * mean_res
    return (mean_now, harm_now)


MESH_ID = pl.DeviceIdType.MESH
LANES = 128
ROWS = 8
F32 = jnp.float32


def swap_bit(pair, stride, bit):
    low, high = pair
    return (
        jnp.where(bit == 0, low, pltpu.roll(high, stride, 1)),
        jnp.where(bit == 0, pltpu.roll(low, LANES - stride, 1), high),
    )


def radial_kernel(
    dims, h_any, m_any, f_ref, w_any, jx_ref, jy_ref, home,
    h_ref, m_ref, w_ref, in_sem, rows, send, recv, mrecv, state, first, omega, mean, mean0, back, own_sem,
    hs_sem, hr_sem, ms_sem, mr_sem, bs_sem, br_sem,
):
    nh, ns, nvar, cells, tiles = dims
    nd = nh * ns
    mh, ms = lax.axis_index("harm"), lax.axis_index("slab")
    me = mh * ns + ms
    nx = ns * cells

    barrier = pltpu.get_barrier_semaphore()

    def flip(index, bits):
        out = index
        weight = 1
        while weight <= bits:
            if bits & weight:
                out = out + weight * (1 - 2 * lax.rem(index // weight, 2))
            weight *= 2
        return out

    def flip_by(index, bits):
        out = index
        weight = 1
        while weight < nh:
            out = out + lax.rem(bits // weight, 2) * weight * (1 - 2 * lax.rem(index // weight, 2))
            weight *= 2
        return out

    def reach(offset):
        oh, os = offset
        return min(oh >> 1, 2) + (oh & 1) + (os >> 1) + 0.3 * (os & 1)

    far_first = sorted(
        [(oh, os) for oh in range(nh) for os in range(ns) if oh or os], key=reach, reverse=True
    )
    for oh, os in far_first:
        pl.semaphore_signal(
            barrier, inc=1, device_id=(flip(mh, oh), flip(ms, os)), device_id_type=MESH_ID
        )
    loads = [
        pltpu.make_async_copy(src, dst, in_sem.at[i])
        for i, (src, dst) in enumerate(((h_any, h_ref), (m_any, m_ref), (w_any, w_ref)))
    ]
    for load in loads:
        load.start()
    for load in loads:
        load.wait()

    lane_all = lax.broadcasted_iota(jnp.int32, (nd, LANES), 1)
    low_bit = lane_all & 1
    high_bit = (lane_all >> 2) & 1

    def place(at, value):
        rows[pl.ds(cells * at, cells), :] = value

    for a in range(nvar):
        for c in range(2):
            place(2 * a + c, h_ref[0, c, a])
    place(2 * nvar, m_ref[nvar - 1])
    place(2 * nvar + 1, w_ref[...].astype(F32))
    for a in range(nvar - 1):
        place(2 * nvar + 2 + a, m_ref[a])

    def block_of(g):
        return g if g < nvar else g + 1

    for grp in range(4):
        mat = jnp.concatenate(
            [rows[ROWS * grp : ROWS * grp + ROWS, LANES * t : LANES * t + LANES] for t in range(tiles)],
            axis=0,
        )
        turned = mat.T
        part = [[turned[nd * (2 * i + j) : nd * (2 * i + j) + nd] for j in range(2)] for i in range(2)]
        cols = [swap_bit((part[0][j], part[1][j]), 4, high_bit) for j in range(2)]
        for g1 in range(2):
            outs = swap_bit((cols[0][g1], cols[1][g1]), 1, low_bit)
            for g0 in range(2):
                send[:, block_of(2 * grp + g1), g0, :] = outs[g0]
    speed = m_ref[1]
    partial_sum = jnp.sum(jnp.sum(speed * speed, axis=1, keepdims=True), axis=0, keepdims=True)
    rate_own = jnp.full((1, 1), 0.25 * f_ref[0].astype(F32), F32)
    send[:, nvar, 0, :] = jnp.broadcast_to(rate_own, (nd, LANES))
    send[:, nvar, 1, :] = jnp.broadcast_to(partial_sum, (nd, LANES))

    recv[mh, ms] = send[me, 0 : nvar + 1]
    mrecv[ms] = send[me, nvar + 1 : nvar + 4]

    pl.semaphore_wait(barrier, nd - 1)

    def out_copy(kd, sd):
        d = kd * ns + sd
        return pltpu.make_async_remote_copy(
            src_ref=send.at[d, pl.ds(0, nvar + 1)],
            dst_ref=recv.at[mh, ms],
            send_sem=hs_sem.at[d],
            recv_sem=hr_sem.at[me],
            device_id=(kd, sd),
            device_id_type=MESH_ID,
        )

    def in_copy(kd, sd):
        d = kd * ns + sd
        return pltpu.make_async_remote_copy(
            src_ref=send.at[d, pl.ds(0, nvar + 1)],
            dst_ref=recv.at[kd, sd],
            send_sem=hs_sem.at[d],
            recv_sem=hr_sem.at[d],
            device_id=(kd, sd),
            device_id_type=MESH_ID,
        )

    def mean_copy(s, slot):
        return pltpu.make_async_remote_copy(
            src_ref=send.at[mh * ns + s, pl.ds(nvar + 1, 3)],
            dst_ref=mrecv.at[slot],
            send_sem=ms_sem.at[s],
            recv_sem=mr_sem.at[slot],
            device_id=(mh, s),
            device_id_type=MESH_ID,
        )

    for oh, os in far_first:
        out_copy(flip(mh, oh), flip(ms, os)).start()
        if oh == 1 and os == ns - 1:
            for o in range(ns - 1, 0, -1):
                mean_copy(flip(ms, o), ms).start()

    lane = lax.broadcasted_iota(jnp.int32, (nx, LANES), 1)
    cell = lax.broadcasted_iota(jnp.int32, (nx, LANES), 0)
    second = (lane >> 1) & 1
    is_real = second == 0

    def other(value):
        return jnp.where(is_real, pltpu.roll(value, LANES - 2, 1), pltpu.roll(value, 2, 1))

    def spread(value):
        turned = other(value)
        return jnp.where(is_real, value, turned), jnp.where(is_real, turned, value)

    for o in range(1, ns):
        peer = flip(ms, o)
        in_copy(mh, peer).wait_recv()
        mean_copy(peer, peer).wait_recv()
    packed = []
    for b in range(3):
        for s in range(ns):
            mean[b, cells * s : cells * s + cells, :] = mrecv[s, b]
        packed.append(mean[b])
    m4, wall = spread(packed[0])
    m0, m1 = spread(packed[1])
    m2, m3 = spread(packed[2])
    for a, value in enumerate((m0, m1, m2, m3, m4)):
        mean[a] = value
        mean0[a] = value
    total = recv[mh, 0, nvar, 1:2, :]
    for s in range(1, ns):
        total = total + recv[mh, s, nvar, 1:2, :]
    count = nx * tiles * LANES
    time_step = jnp.broadcast_to(0.9 / (1.0 + jnp.sqrt(total / count)), (nx, LANES))
    wall2 = 2.0 * wall
    z = (lane & 1) * nd + me
    radius = 0.5 + (z.astype(F32) + 0.5) / (2 * nd)
    inv_r = 1.0 / radius

    mp1 = jnp.where(cell < nx - 1, 1.0, 0.0).astype(F32)
    mm1 = jnp.where(cell > 0, 1.0, 0.0).astype(F32)
    mp2 = jnp.where(cell < nx - 2, 1.0, 0.0).astype(F32)
    mm2 = jnp.where(cell > 1, 1.0, 0.0).astype(F32)

    def xp(v, n):
        return pltpu.roll(v, nx - n, 0)

    def xm(v, n):
        return pltpu.roll(v, n, 0)

    def yp(v, n):
        return pltpu.roll(v, LANES - 4 * n, 1)

    def ym(v, n):
        return pltpu.roll(v, 4 * n, 1)

    def pieces(v, fwd, bwd):
        xp1, xm1 = xp(v, 1), xm(v, 1)
        yp1, ym1 = yp(v, 1), ym(v, 1)
        fourth = (
            mp2 * xp(v, 2) + mm2 * xm(v, 2) + 12.0 * v + yp(v, 2) + ym(v, 2)
            - 4.0 * (mp1 * xp1 + mm1 * xm1 + yp1 + ym1)
        )
        return fwd * xp1 - bwd * xm1, yp1 - ym1, fourth

    def mix(us, vs, a):
        flux = jx_ref[a, 0] * us[0]
        for b in range(1, nvar):
            flux = flux + jx_ref[a, b] * us[b]
        for b in range(nvar):
            flux = flux + jy_ref[a, b] * vs[b]
        return 0.5 * flux

    pairs = ((1, 1), (1, 2), (1, 3), (2, 2), (2, 3), (3, 3), (4, 1), (4, 2), (4, 3))

    zero = jnp.zeros((nx, LANES), F32)
    empty = (zero,) * len(pairs)

    def products(acc, hs):
        return tuple(s + hs[p] * hs[q] for s, (p, q) in zip(acc, pairs))

    def advance(k, hs, om, edges, step):
        om = jnp.where(is_real, om, -om)
        got = [pieces(h, *edges) for h in hs]
        us, vs = [g[0] for g in got], [g[1] for g in got]
        news = []
        for a in range(nvar):
            res = om * other(hs[a]) - mix(us, vs, a) - 0.05 * got[a][2] - wall2 * hs[a]
            news.append(first[k, a] + step * res)
        return news

    def edges_of(mc):
        return mp1 * xp(mc, 1), mm1 * xm(mc, 1)

    def gx(v):
        return 0.5 * (mp1 * xp(v, 1) - mm1 * xm(v, 1))

    def gy(v):
        return 0.5 * (yp(v, 1) - ym(v, 1))

    def advance_mean(acc, step):
        s = [0.5 * (v + other(v)) for v in acc]
        force = (
            zero,
            -gx(s[0]) - gy(s[1]),
            -gx(s[1]) - gy(s[3]) - 2.0 * s[4] * inv_r,
            -gx(s[2]) - gy(s[4]) + (s[3] - s[5]) * inv_r,
            -gx(s[6]) - gy(s[7]) - s[8] * inv_r,
        )
        got = [pieces(mean[a], mp1, mm1) for a in range(nvar)]
        us, vs = [g[0] for g in got], [g[1] for g in got]
        for a in range(nvar):
            res = force[a] - mix(us, vs, a) - 0.05 * got[a][2]
            mean[a] = mean0[a] + step * res

    edges = edges_of(mean[1])
    step = SECTION_RATES[0] * time_step

    def landed(k, accs):
        before, after = accs
        for s in range(ns):
            for a in range(nvar):
                first[k, a, cells * s : cells * s + cells, :] = recv[k, s, a]
        om = jnp.broadcast_to(recv[k, 0, nvar, 0:1, :], (nx, LANES))
        omega[k] = om
        hs = [first[k, a] for a in range(nvar)]
        news = advance(k, hs, om, edges, step)
        for a in range(nvar):
            state[k, a] = news[a]
        return products(before, hs), products(after, news)

    def arrive(o, accs):
        k = flip_by(mh, o)
        for os in range(ns):
            in_copy(k, flip(ms, os)).wait_recv()
        return landed(k, accs)

    before, acc = lax.fori_loop(1, nh, arrive, landed(mh, (empty, empty)), unroll=nh - 1)
    advance_mean(before, step)

    def section(i, acc):
        step = jnp.where(i == 1, SECTION_RATES[1], SECTION_RATES[2]).astype(F32) * time_step
        edges = edges_of(mean[1])

        def one(k, after):
            news = advance(k, [state[k, a] for a in range(nvar)], omega[k], edges, step)
            for a in range(nvar):
                state[k, a] = news[a]
            return products(after, news)

        after = lax.fori_loop(0, nh, one, empty, unroll=nh)
        advance_mean(acc, step)
        return after

    acc = lax.fori_loop(1, 3, section, acc)

    step = SECTION_RATES[3] * time_step
    edges = edges_of(mean[1])
    advance_mean(acc, step)

    def join(even, odd):
        return jnp.where(is_real, even, odd)

    packs = (mean[4], join(mean[0], mean[1]), join(mean[2], mean[3]))

    def back_copy(k, s, slot):
        d = k * ns + s
        return pltpu.make_async_remote_copy(
            src_ref=back.at[k, s],
            dst_ref=home.at[slot],
            send_sem=bs_sem.at[d],
            recv_sem=br_sem.at[slot],
            device_id=(k, s),
            device_id_type=MESH_ID,
        )

    def finish(k):
        news = advance(k, [state[k, a] for a in range(nvar)], omega[k], edges, step)
        for s in range(ns):
            for a in range(nvar):
                back[k, s, a] = news[a][cells * s : cells * s + cells, :]
            for b in range(3):
                back[k, s, nvar + b] = packs[b][cells * s : cells * s + cells, :]

    def depart(o, _):
        k = flip_by(mh, nh - 1 - o)
        finish(k)
        for os in range(ns - 1, -1, -1):
            back_copy(k, flip(ms, os), me).start()
        return 0

    lax.fori_loop(0, nh - 1, depart, 0, unroll=nh - 1)
    finish(mh)
    for os in range(ns - 1, 0, -1):
        back_copy(mh, flip(ms, os), me).start()
    own = pltpu.make_async_copy(back.at[mh, ms], home.at[me], own_sem)
    own.start()

    def land_back(o, _):
        d = lax.rem(me + o, nd)
        back_copy(d // ns, lax.rem(d, ns), d).wait_recv()
        return 0

    lax.fori_loop(1, nd, land_back, 0)

    own.wait()

    def sent(o, _):
        d = lax.rem(me + o, nd)
        out_copy(d // ns, lax.rem(d, ns)).wait_send()
        back_copy(d // ns, lax.rem(d, ns), me).wait_send()
        return 0

    lax.fori_loop(1, nd, sent, 0)
    for o in range(1, ns):
        mean_copy(flip(ms, o), ms).wait_send()


def gather_kernel(dims, home, mo_ref, ho_ref, rows):
    nh, ns, nvar, cells, tiles = dims
    nd = nh * ns
    lane_all = lax.broadcasted_iota(jnp.int32, (nd, LANES), 1)
    low_bit = lane_all & 1
    high_bit = (lane_all >> 2) & 1

    for grp in range(4):
        cols = []
        for g1 in range(2):
            cols.append(swap_bit([home[:, 2 * grp + g1, g0, :] for g0 in range(2)], 1, low_bit))
        part = [swap_bit((cols[0][j], cols[1][j]), 4, high_bit) for j in range(2)]
        mat = jnp.concatenate([part[j][i] for i in range(2) for j in range(2)], axis=0)
        turned = mat.T
        for t in range(tiles):
            rows[ROWS * grp : ROWS * grp + ROWS, LANES * t : LANES * t + LANES] = turned[
                ROWS * t : ROWS * t + ROWS
            ]

    def take(at):
        return rows[pl.ds(cells * at, cells), :]

    for a in range(nvar):
        for c in range(2):
            ho_ref[0, c, a] = take(2 * a + c)
    mo_ref[nvar - 1] = take(2 * nvar)
    for a in range(nvar - 1):
        mo_ref[a] = take(2 * nvar + 2 + a)


def radial_shards(nh, ns, harmonics, mean_flow, freq_index, wall_mask, jacobian_x, jacobian_y):
    nvar, cells, planes = mean_flow.shape
    nd, nx = nh * ns, ns * cells
    vmem = pl.BlockSpec(memory_space=pltpu.VMEM)
    smem = pl.BlockSpec(memory_space=pltpu.SMEM)
    anywhere = pl.BlockSpec(memory_space=pl.ANY)
    dims = (nh, ns, nvar, cells, planes // LANES)
    field = (nx, LANES)
    piece = (cells, LANES)
    home = pl.pallas_call(
        functools.partial(radial_kernel, dims),
        out_shape=jax.ShapeDtypeStruct((nd, nvar + 3, *piece), F32),
        in_specs=[anywhere, anywhere, smem, anywhere, smem, smem],
        out_specs=anywhere,
        scratch_shapes=[
            pltpu.VMEM(harmonics.shape, F32),
            pltpu.VMEM(mean_flow.shape, F32),
            pltpu.VMEM(wall_mask.shape, jnp.int32),
            pltpu.SemaphoreType.DMA((3,)),
            pltpu.VMEM((4 * ROWS, planes), F32),
            pltpu.VMEM((nd, nvar + 4, *piece), F32),
            pltpu.VMEM((nh, ns, nvar + 1, *piece), F32),
            pltpu.VMEM((ns, 3, *piece), F32),
            pltpu.VMEM((nh, nvar, *field), F32),
            pltpu.VMEM((nh, nvar, *field), F32),
            pltpu.VMEM((nh, *field), F32),
            pltpu.VMEM((nvar, *field), F32),
            pltpu.VMEM((nvar, *field), F32),
            pltpu.VMEM((nh, ns, nvar + 3, *piece), F32),
            pltpu.SemaphoreType.DMA,
            pltpu.SemaphoreType.DMA((nd,)),
            pltpu.SemaphoreType.DMA((nd,)),
            pltpu.SemaphoreType.DMA((ns,)),
            pltpu.SemaphoreType.DMA((ns,)),
            pltpu.SemaphoreType.DMA((nd,)),
            pltpu.SemaphoreType.DMA((nd,)),
        ],
        compiler_params=pltpu.CompilerParams(collective_id=0, has_side_effects=True),
    )(harmonics, mean_flow, freq_index, wall_mask, jacobian_x, jacobian_y)
    return pl.pallas_call(
        functools.partial(gather_kernel, dims),
        out_shape=(
            jax.ShapeDtypeStruct(mean_flow.shape, F32),
            jax.ShapeDtypeStruct(harmonics.shape, F32),
        ),
        in_specs=[vmem],
        out_specs=(vmem, vmem),
        scratch_shapes=[pltpu.VMEM((4 * ROWS, planes), F32)],
    )(home)


def fits_radial(nh, ns, harmonics, mean_flow):
    owned, parts, nvar, cells, planes = harmonics.shape
    return (
        NZ == 2 * nh * ns
        and LANES == 2 * NZ
        and (owned, parts, nvar, cells) == (1, 2, 5, 2)
        and ns * cells == ROWS
        and planes == 16 * LANES
    )


def either(nh, ns, harmonics, mean_flow, *rest):
    if fits_radial(nh, ns, harmonics, mean_flow):
        return radial_shards(nh, ns, harmonics, mean_flow, *rest)
    return shards(harmonics, mean_flow, *rest)


def solution(mesh):
    placed = (
        P("harm", None, None, "slab", None),
        P(None, "slab", None),
        P("harm"),
        P("slab", None),
        P(),
        P(),
    )
    return jax.shard_map(
        functools.partial(either, mesh.shape["harm"], mesh.shape["slab"]),
        mesh=mesh,
        in_specs=placed,
        out_specs=(P(None, "slab", None), P("harm", None, None, "slab", None)),
        check_vma=False,
    )
```
